32 devices in a mesh: wide: 8 (over y, x, core), narrow: 4 (over z).
Axes of the slice: x: 2, y: 2, z: 4, core: 2. Of those that a mesh axis runs over, the one named last changes fastest.
Arguments:
- stream: bfloat16 [8192, 2048], P('wide', 'narrow'), may hold values from -10 to 10
- chain_ids: int32 [8192], P('wide'), may hold values from 0 to 20, as said below
- valid_slots: int32 [8192], P('wide'), may hold values from 0 to 1, as said below
- w_qkv: bfloat16 [3, 2048, 2048], P(None, 'wide', 'narrow'), may hold values from -0.125 to 0.125
- b_qkv: float32 [3, 2048], P(None, 'narrow'), may hold values from -3 to 3
- w_out: bfloat16 [2048, 2048], P('narrow', 'wide'), may hold values from -3 to 3
- gain_one: float32 [2048], P('narrow'), may hold values from 0.5 to 1.5
- bias_one: float32 [2048], P('narrow'), may hold values from -3 to 3
- w_up: bfloat16 [2048, 2, 5504], P('wide', None, 'narrow'), may hold values from -0.125 to 0.125
- w_down: bfloat16 [5504, 2048], P('narrow', 'wide'), may hold values from -0.4375 to 0.4375
- gain_two: float32 [2048], P('narrow'), may hold values from 0.5 to 1.5
- bias_two: float32 [2048], P('narrow'), may hold values from -3 to 3
- cotangent: bfloat16 [8192, 2048], P('wide', 'narrow'), may hold values from -6 to 6
Outputs:
- output: bfloat16 [8192, 2048], P('wide', 'narrow')
- grad_stream: bfloat16 [8192, 2048], P('wide', 'narrow')
- grad_qkv_weight: float32 [3, 2048, 2048], P(None, 'wide', 'narrow')
- grad_qkv_bias: float32 [3, 2048], P(None, 'narrow')
- grad_out_weight: float32 [2048, 2048], P('narrow', 'wide')
- grad_gain_one: float32 [2048], P('narrow')
- grad_bias_one: float32 [2048], P('narrow')
- grad_up_weight: float32 [2048, 2, 5504], P('wide', None, 'narrow')
- grad_down_weight: float32 [5504, 2048], P('narrow', 'wide')
- grad_gain_two: float32 [2048], P('narrow')
- grad_bias_two: float32 [2048], P('narrow')
- stream_stats: float32 [3], replicated
The draws below stay inside these ranges and needn't reach their ends.
Inputs may be any that keep to these rules, and one draw needn't show every extreme that they name: `chain_ids`: within each row of 1024 slots the chain numbers start at 0 and never fall; every chain but a row's last holds at least 50 slots; in the first row every chain but the last holds exactly 50 slots. `valid_slots`: in each row of 1024 slots the ones form a prefix of at least 768 slots.
All inputs are finite; a program needn't handle non-finite values.
Results may differ from the reference program's by a relative error of at most 0.019.
Values may be sent and summed in bfloat16 or wider, within the bound.
A program may use at most 192 MiB of HBM per device.

```python
import math
import jax
import jax.numpy as jnp
from jax import lax

D = 2048
HEAD_DIM = 128
FF = 5461
FF_PAD = 5504
TOK_DEV = 1024
MIN_CHAIN = 50
MAX_CHAIN = 1024
TOKENS = 8192


def chain_layout(key):
    row_count = TOKENS // TOK_DEV
    most_chains = TOK_DEV // MIN_CHAIN + 1
    length_key = jax.random.fold_in(key, 11)
    live_key = jax.random.fold_in(key, 12)
    lengths = jax.random.randint(length_key, (row_count, most_chains), MIN_CHAIN, MAX_CHAIN + 1)
    first_row = (jnp.arange(row_count, dtype=jnp.int32) == 0)[:, None]
    lengths = jnp.where(first_row, MIN_CHAIN, lengths).astype(jnp.int32)
    chain_ends = jnp.cumsum(lengths, axis=1)
    slot_index = jnp.arange(TOK_DEV, dtype=jnp.int32)
    chains = jnp.sum((chain_ends[:, None, :] <= slot_index[None, :, None]).astype(jnp.int32), axis=2)
    live_count = jax.random.randint(live_key, (row_count, 1), 3 * TOK_DEV // 4, TOK_DEV + 1)
    live = (slot_index[None, :] < live_count).astype(jnp.int32)
    return (chains.reshape(TOKENS).astype(jnp.int32), live.reshape(TOKENS))


def draw_chain_ids(key, part):
    chains, live = chain_layout(key)
    return chains


def draw_valid_slots(key, part):
    chains, live = chain_layout(key)
    return live


def draw_stream(key, part):
    row_key = jax.random.fold_in(key, 21)
    entry_key = jax.random.fold_in(key, 22)
    place = jnp.arange(TOKENS, dtype=jnp.float32) / TOKENS
    jitter = jnp.exp(jax.random.uniform(row_key, (TOKENS, 1), minval=-0.22, maxval=0.22))
    entries = jnp.clip(jax.random.normal(entry_key, (TOKENS, D)), -5.0, 5.0)
    return (entries * (0.5 + place[:, None]) * jitter).astype(jnp.bfloat16)


def block_levels(rng, dims, cuts, low, high):
    def one(dim, parts):
        steps = jax.random.uniform(jax.random.fold_in(jax.random.fold_in(rng, 6), dim), (parts,), jnp.float32, low / len(cuts), high / len(cuts))
        return jnp.repeat(jnp.exp(steps), dims[dim] // parts).reshape((-1,) + (1,) * (len(dims) - dim - 1))

    level = one(*cuts[0])
    for cut in cuts[1:]:
        level = level * one(*cut)
    return level


def gaussian(stream_key, shape, scale, bound, pieces=(), kind=jnp.bfloat16):
    loudness = block_levels(stream_key, shape, pieces, -0.22, 0.18) if pieces else 1.0
    values = jax.random.normal(stream_key, shape, jnp.float32) * scale * loudness
    return jnp.minimum(jnp.maximum(values, -bound), bound).astype(kind)


def setup_inputs(seed: int = 0) -> dict:
    streams_of = jax.random.split(jax.random.key(seed), 14)
    return {
        "stream": draw_stream(jax.random.fold_in(streams_of[13], 71), 0),
        "chain_ids": draw_chain_ids(jax.random.fold_in(streams_of[13], 71), 0),
        "valid_slots": draw_valid_slots(jax.random.fold_in(streams_of[13], 71), 0),
        "w_qkv": gaussian(streams_of[3], (3, D, D), D ** -0.5, 0.125, ((1, 8), (2, 4))),
        "b_qkv": gaussian(streams_of[4], (3, D), 0.5, 3.0, ((1, 4),), jnp.float32),
        "w_out": gaussian(streams_of[5], (D, D), 4 ** -0.5, 3.0, ((0, 4), (1, 8))),
        "gain_one": jnp.clip(1.0 + 0.1 * jax.random.normal(streams_of[6], (D,), jnp.float32), 0.5, 1.5),
        "bias_one": gaussian(streams_of[7], (D,), 0.5, 3.0, ((0, 4),), jnp.float32),
        "w_up": gaussian(streams_of[8], (D, 2, FF_PAD), D ** -0.5, 0.125, ((0, 8), (2, 4))),
        "w_down": gaussian(streams_of[9], (FF_PAD, D), (FF // 32) ** -0.5, 0.4375, ((0, 4), (1, 8))),
        "gain_two": jnp.clip(1.0 + 0.1 * jax.random.normal(streams_of[10], (D,), jnp.float32), 0.5, 1.5),
        "bias_two": gaussian(streams_of[11], (D,), 0.5, 3.0, ((0, 4),), jnp.float32),
        "cotangent": gaussian(streams_of[12], (TOKENS, D), 1.0, 6.0, ((0, 8), (1, 4))),
    }


@jax.custom_vjp
def low(v):
    return lax.optimization_barrier(v.astype(jnp.bfloat16)).astype(jnp.float32)

@jax.custom_vjp
def low_back(v):
    return v

def low_keep(v):
    return (low(v), None)

def low_pass(kept, grad):
    return (grad,)

def back_keep(v):
    return (v, None)

def back_low(kept, grad):
    return (low(grad),)
low.defvjp(low_keep, low_pass)
low_back.defvjp(back_keep, back_low)
deep_alpha = 6.928203230275509
norm_eps = 1e-05
mask_value = -1e+30
rope_base = 10000.0
precise = lax.Precision.HIGHEST

def positions_of(chain_row):
    slot_index = jnp.arange(chain_row.shape[0], dtype=jnp.int32)
    same_chain = chain_row[:, None] == chain_row[None, :]
    earlier = slot_index[None, :] < slot_index[:, None]
    return lax.optimization_barrier(jnp.sum(jnp.where(same_chain & earlier, 1, 0), axis=1)).astype(jnp.int32)

def rotary_tables(positions):
    half_dim = HEAD_DIM // 2
    frequency = rope_base ** (-2.0 * jnp.arange(half_dim, dtype=jnp.float32) / HEAD_DIM)
    angles = positions.astype(jnp.float32)[:, None] * frequency[None, :]
    return (jnp.cos(angles), jnp.sin(angles))

def rotate(values, cosine, sine):
    half_dim = values.shape[-1] // 2
    first_half = values[..., :half_dim]
    second_half = values[..., half_dim:]
    cos_part = cosine[:, None, :]
    sin_part = sine[:, None, :]
    return jnp.concatenate([first_half * cos_part - second_half * sin_part, second_half * cos_part + first_half * sin_part], axis=-1)

def layer_norm(resid, gain, bias):
    centre = lax.optimization_barrier(jnp.mean(resid, axis=-1, keepdims=True))
    centred = resid - centre
    spread = lax.optimization_barrier(jnp.mean(centred * centred, axis=-1, keepdims=True))
    return centred * lax.rsqrt(spread + norm_eps) * gain + bias

def attend_pack(packed):
    query, keys_in, value, chain_row, live_row = packed
    score_scale = 1.0 / math.sqrt(HEAD_DIM)
    scores = low_back(jnp.einsum('qhd,khd->hqk', query, keys_in, precision=precise) * score_scale)
    allowed = (live_row[None, :] > 0) & ((chain_row[:, None] == chain_row[None, :]) | (live_row[:, None] == 0))
    scores = jnp.where(allowed[None], scores, mask_value)
    row_top = lax.optimization_barrier(jnp.max(scores, axis=-1, keepdims=True))
    weights = jnp.exp(scores - row_top)
    probability = weights / lax.optimization_barrier(jnp.sum(weights, axis=-1, keepdims=True))
    return jnp.einsum('hqk,khd->qhd', low(probability), value, precision=precise)

def forward(stream_full, w_qkv, b_qkv, w_out, gain_one, bias_one, w_up, w_down, gain_two, bias_two, chain_rows, live_rows, cosine, sine):
    tokens = stream_full.shape[0]
    width = stream_full.shape[1]
    heads = width // HEAD_DIM
    row_count = chain_rows.shape[0]
    unit_mask = (jnp.arange(FF_PAD) < FF).astype(jnp.float32)
    proj = jnp.einsum('td,cde->cte', stream_full, w_qkv, precision=precise) + b_qkv[:, None, :]
    proj = low_back(proj).reshape(3, tokens, heads, HEAD_DIM)
    query = low(rotate(proj[0], cosine, sine))
    keys_all = low(rotate(proj[1], cosine, sine))
    value = low(proj[2])

    def by_rows(values):
        return values.reshape(row_count, tokens // row_count, heads, HEAD_DIM)
    mixed = lax.map(jax.checkpoint(attend_pack), (by_rows(query), by_rows(keys_all), by_rows(value), chain_rows, live_rows))
    mixed = low_back(low(mixed.reshape(tokens, width)))
    branch = low_back(jnp.dot(mixed, w_out, precision=precise))
    resid_one = deep_alpha * stream_full + branch
    normed = layer_norm(resid_one, gain_one, bias_one)
    gate_up = low_back(jnp.einsum('td,dcf->tcf', low(normed), w_up * unit_mask, precision=precise))
    hidden = low(jax.nn.gelu(gate_up[:, 0], approximate=True) * gate_up[:, 1])
    ffn = low_back(jnp.dot(hidden, w_down * unit_mask[:, None], precision=precise))
    resid_two = deep_alpha * normed + ffn
    return (layer_norm(resid_two, gain_two, bias_two), (resid_one, branch, ffn))

def reference(stream, chain_ids, valid_slots, w_qkv, b_qkv, w_out, gain_one, bias_one, w_up, w_down, gain_two, bias_two, cotangent):
    row_count = TOKENS // TOK_DEV
    chain_rows = chain_ids.reshape(row_count, TOK_DEV)
    live_rows = valid_slots.reshape(row_count, TOK_DEV)
    positions = lax.map(positions_of, chain_rows).reshape(TOKENS)
    cosine, sine = rotary_tables(positions)
    live = valid_slots.astype(jnp.float32)
    floats = (stream.astype(jnp.float32), w_qkv.astype(jnp.float32), b_qkv.astype(jnp.float32), w_out.astype(jnp.float32), gain_one.astype(jnp.float32), bias_one.astype(jnp.float32), w_up.astype(jnp.float32), w_down.astype(jnp.float32), gain_two.astype(jnp.float32), bias_two.astype(jnp.float32))

    def layer(*values):
        return forward(*values, chain_rows, live_rows, cosine, sine)
    output, pullback, kept = jax.vjp(layer, *floats, has_aux=True)
    grads = pullback(cotangent.astype(jnp.float32) * live[:, None])
    resid_one, branch, ffn = kept
    live_col = live[:, None]
    squares = jnp.stack([jnp.sum(live_col * resid_one * resid_one), jnp.sum(live_col * branch * branch), jnp.sum(live_col * ffn * ffn)])
    count = jnp.sum(live) * D
    stream_stats = jnp.sqrt(squares / count)
    return (output.astype(jnp.bfloat16), grads[0].astype(jnp.bfloat16), grads[1], grads[2], grads[3], grads[4], grads[5], grads[6], grads[7], grads[8], grads[9], stream_stats)
```

```python
import functools
import math

import jax
import jax.numpy as jnp
import numpy as np
from jax import lax
from jax.experimental import pallas as pl
from jax.experimental.pallas import tpu as pltpu
from jax.sharding import Mesh
from jax.sharding import PartitionSpec as P

HEAD_DIM = 128
FF = 5461

deep_alpha = 6.928203230275509
norm_eps = 1e-05
mask_value = -1e30
rope_base = 10000.0
score_scale = 1.0 / math.sqrt(HEAD_DIM)

f32 = jnp.float32
bf16 = jnp.bfloat16
SWAP = [(0, 1), (1, 0)]


def swap(values, axis):
    return lax.ppermute(values, axis, SWAP)


def qkv_kernel(s_ref, w_ref, b_ref, cos_ref, sin_ref, q_ref, k_ref, v_ref):
    rows = s_ref[...]
    cos, sin = cos_ref[...], sin_ref[...]
    for c, out in enumerate((q_ref, k_ref, v_ref)):
        acc = jnp.dot(rows, w_ref[c], preferred_element_type=f32) + b_ref[c : c + 1, :]
        if c == 2:
            out[...] = acc.astype(bf16)
            continue
        for h in range(acc.shape[1] // HEAD_DIM):
            cols = slice(h * HEAD_DIM, (h + 1) * HEAD_DIM)
            head = acc[:, cols]
            turned = pltpu.roll(head, HEAD_DIM // 2, 1)
            out[:, cols] = (head * cos + turned * sin).astype(bf16)


def qkv_project(stream_row, weight, bias, cos, sin):
    tokens, depth = stream_row.shape
    cols = weight.shape[2]
    tile = 256
    shape = jax.ShapeDtypeStruct((tokens, cols), bf16)
    return pl.pallas_call(
        qkv_kernel,
        grid=(tokens // tile,),
        in_specs=[
            pl.BlockSpec((tile, depth), lambda i: (i, 0)),
            pl.BlockSpec((3, depth, cols), lambda i: (0, 0, 0)),
            pl.BlockSpec((3, cols), lambda i: (0, 0)),
            pl.BlockSpec((tile, HEAD_DIM), lambda i: (i, 0)),
            pl.BlockSpec((tile, HEAD_DIM), lambda i: (i, 0)),
        ],
        out_specs=[pl.BlockSpec((tile, cols), lambda i: (i, 0))] * 3,
        out_shape=[shape] * 3,
        name="qkv_project",
        cost_estimate=pl.CostEstimate(
            flops=2 * tokens * depth * 3 * cols,
            bytes_accessed=2 * (tokens * depth + 3 * depth * cols + 3 * tokens * cols),
            transcendentals=0,
        ),
    )(stream_row, weight, bias, cos, sin)


def allowed_of(key_code, query_code):
    return (key_code == query_code) | ((query_code < 0) & (key_code >= 0))


def attend_kernel(q_ref, k_ref, v_ref, kc_ref, qc_ref, o_ref, lse_ref):
    scores = lax.dot_general(
        k_ref[...], q_ref[...], (((1,), (1,)), ((), ())), preferred_element_type=f32
    )
    scores = jnp.where(allowed_of(kc_ref[...], qc_ref[...]), scores * score_scale, mask_value)
    top = jnp.max(scores, axis=0, keepdims=True)
    weights = jnp.exp(scores - top)
    total = jnp.sum(weights, axis=0, keepdims=True)
    mixed = lax.dot_general(
        v_ref[...], weights.astype(bf16), (((0,), (0,)), ((), ())), preferred_element_type=f32
    )
    o_ref[...] = jnp.transpose(mixed / total).astype(bf16)
    lse_ref[0] = top + jnp.log(total)


def attend(query, keys, value, key_code, query_code):
    tokens, cols = query.shape
    heads = cols // HEAD_DIM
    tile = 256
    per_q = pl.BlockSpec((tile, HEAD_DIM), lambda h, i: (i, h))
    per_head = pl.BlockSpec((tokens, HEAD_DIM), lambda h, i: (0, h))
    return pl.pallas_call(
        attend_kernel,
        grid=(heads, tokens // tile),
        in_specs=[
            per_q,
            per_head,
            per_head,
            pl.BlockSpec((tokens, 1), lambda h, i: (0, 0)),
            pl.BlockSpec((1, tile), lambda h, i: (0, i)),
        ],
        out_specs=[per_q, pl.BlockSpec((1, 1, tile), lambda h, i: (h, 0, i))],
        out_shape=[
            jax.ShapeDtypeStruct((tokens, cols), bf16),
            jax.ShapeDtypeStruct((heads, 1, tokens), f32),
        ],
        name="attend",
        cost_estimate=pl.CostEstimate(
            flops=4 * tokens * tokens * cols,
            bytes_accessed=8 * tokens * cols,
            transcendentals=heads * tokens * tokens,
        ),
    )(query, keys, value, key_code, query_code)


def attend_back_kernel(
    q_ref, k_ref, v_ref, g_ref, kc_ref, qc_ref, lse_ref, cosq_ref, sinq_ref, cosk_ref, sink_ref,
    dq_ref, dk_ref, dv_ref, dk_acc, dv_acc,
):
    step = pl.program_id(1)

    @pl.when(step == 0)
    def _():
        dk_acc[...] = jnp.zeros_like(dk_acc)
        dv_acc[...] = jnp.zeros_like(dv_acc)

    query, keys, grads = q_ref[...], k_ref[...], g_ref[...]
    nt = (((1,), (1,)), ((), ()))
    scores = lax.dot_general(keys, query, nt, preferred_element_type=f32)
    scores = jnp.where(allowed_of(kc_ref[...], qc_ref[...]), scores * score_scale, mask_value)
    probs = jnp.exp(scores - lse_ref[0])
    grad_probs = lax.dot_general(v_ref[...], grads, nt, preferred_element_type=f32)
    mean = jnp.sum(probs * grad_probs, axis=0, keepdims=True)
    grad_scores = (probs * (grad_probs - mean)).astype(bf16)
    dv_acc[...] += jnp.dot(probs.astype(bf16), grads, preferred_element_type=f32)
    dk_acc[...] += jnp.dot(grad_scores, query, preferred_element_type=f32)
    dq = jnp.transpose(
        lax.dot_general(keys, grad_scores, (((0,), (0,)), ((), ())), preferred_element_type=f32)
    )
    dq = dq * score_scale
    half = HEAD_DIM // 2
    dq_ref[...] = (dq * cosq_ref[...] - pltpu.roll(dq, half, 1) * sinq_ref[...]).astype(bf16)

    @pl.when(step == pl.num_programs(1) - 1)
    def _():
        dk = dk_acc[...] * score_scale
        dk_ref[...] = (dk * cosk_ref[...] - pltpu.roll(dk, half, 1) * sink_ref[...]).astype(bf16)
        dv_ref[...] = dv_acc[...].astype(bf16)


def attend_back(query, keys, value, grad_mixed, key_code, query_code, lse, cos, sin):
    tokens, cols = query.shape
    heads = cols // HEAD_DIM
    tile = 256
    per_q = pl.BlockSpec((tile, HEAD_DIM), lambda h, i: (i, h))
    per_head = pl.BlockSpec((tokens, HEAD_DIM), lambda h, i: (0, h))
    table_q = pl.BlockSpec((tile, HEAD_DIM), lambda h, i: (i, 0))
    table = pl.BlockSpec((tokens, HEAD_DIM), lambda h, i: (0, 0))
    return pl.pallas_call(
        attend_back_kernel,
        grid=(heads, tokens // tile),
        in_specs=[
            per_q,
            per_head,
            per_head,
            per_q,
            pl.BlockSpec((tokens, 1), lambda h, i: (0, 0)),
            pl.BlockSpec((1, tile), lambda h, i: (0, i)),
            pl.BlockSpec((1, 1, tile), lambda h, i: (h, 0, i)),
            table_q,
            table_q,
            table,
            table,
        ],
        out_specs=[per_q, per_head, per_head],
        out_shape=[jax.ShapeDtypeStruct((tokens, cols), bf16)] * 3,
        scratch_shapes=[pltpu.VMEM((tokens, HEAD_DIM), f32)] * 2,
        name="attend_back",
        cost_estimate=pl.CostEstimate(
            flops=10 * tokens * tokens * cols,
            bytes_accessed=14 * tokens * cols,
            transcendentals=heads * tokens * tokens,
        ),
    )(query, keys, value, grad_mixed, key_code, query_code, lse, cos, sin, cos, sin)


def by_core(mine, other, axis):
    first = jnp.concatenate([mine, other], axis=axis)
    second = jnp.concatenate([other, mine], axis=axis)
    return jnp.where(lax.axis_index("core") == 0, first, second)


def halves_by_core(values, axis):
    size = values.shape[axis] // 2
    c = lax.axis_index("core")
    return (
        lax.dynamic_slice_in_dim(values, c * size, size, axis),
        lax.dynamic_slice_in_dim(values, (1 - c) * size, size, axis),
    )


def core_exchange(shard, axis_units, axis_rows):
    keep, give = halves_by_core(shard, axis_units)
    return by_core(keep, swap(give, "core"), axis_rows)


def core_return(piece, axis_units, axis_rows):
    keep, give = halves_by_core(piece, axis_rows)
    return by_core(keep, swap(give, "core"), axis_units)


def plane_gather(piece, axis, plane):
    return lax.all_gather(piece, plane, axis=axis, tiled=True)


def plane_scatter(product, axis, plane):
    return lax.psum_scatter(product, plane, scatter_dimension=axis, tiled=True)


def added(*terms):
    total = terms[0].astype(f32)
    for term in terms[1:]:
        total = total + term.astype(f32)
    return total


def after(values, *earlier):
    return lax.optimization_barrier((values, *earlier))[0]


def team_gather(own):
    core = swap(own, "core")
    chip = swap(own, "zl")
    return (
        jnp.concatenate([own, core], axis=0),
        jnp.concatenate([chip, swap(chip, "core")], axis=0),
    )


def team_scatter(near, far):
    share = far.shape[0] // 2
    far_sum = added(far[:share], swap(far[share:].astype(bf16), "core")).astype(bf16)
    from_chip = swap(far_sum, "zl")
    from_core = swap(near[share:].astype(bf16), "core")
    return added(near[:share], from_core, from_chip)


TEAM = ("core", "zh", "zl")


def team_index(c, zh, zl):
    return c * 4 + zh * 2 + zl


def to_team(k1, k2):
    return [
        (team_index(c, h, q), team_index(h ^ k1, c, q ^ k2))
        for c in (0, 1)
        for h in (0, 1)
        for q in (0, 1)
    ]


def from_team(k1, k2):
    return [(b, a) for a, b in to_team(k1, k2)]


CORNERS = [(0, 0), (0, 1), (1, 0), (1, 1)]


def layer_norm(resid):
    centred = resid - jnp.mean(resid, axis=1, keepdims=True)
    inverse = lax.rsqrt(jnp.mean(centred * centred, axis=1, keepdims=True) + norm_eps)
    return centred * inverse, inverse


def norm_backward(grad_in, unit, inverse, gain):
    grad_unit = grad_in * gain
    first = jnp.mean(grad_unit, axis=1, keepdims=True)
    second = jnp.mean(grad_unit * unit, axis=1, keepdims=True)
    grad_resid = inverse * (grad_unit - first - unit * second)
    return grad_resid, jnp.sum(grad_in * unit, axis=0), jnp.sum(grad_in, axis=0)


def gelu_parts(gate):
    root = math.sqrt(2.0 / math.pi)
    inner = jnp.tanh(root * (gate + 0.044715 * gate * gate * gate))
    half = 0.5 * (1.0 + inner)
    slope = half + 0.5 * gate * (1.0 - inner * inner) * root * (1.0 + 3 * 0.044715 * gate * gate)
    return gate * half, slope


def nt(a, b):
    return lax.dot_general(a, b, (((1,), (1,)), ((), ())), preferred_element_type=f32)


def nn(a, b):
    return jnp.dot(a, b, preferred_element_type=f32)


def tn(a, b):
    return lax.dot_general(a, b, (((0,), (0,)), ((), ())), preferred_element_type=f32)


def body(
    square,
    stream,
    chain_ids,
    valid_slots,
    w_qkv,
    b_qkv,
    w_out,
    gain_one,
    bias_one,
    w_up,
    w_down,
    gain_two,
    bias_two,
    cotangent,
):
    c, zh, zl = (lax.axis_index(a) for a in TEAM)
    tokens, quarter = stream.shape
    width = quarter * 4
    share = tokens // 4
    plane = ("y", "x") if square else ("plane",)
    units_here = w_down.shape[0] // 2

    def block_order(parts, key):
        size = parts[0].shape[-1]
        out = jnp.zeros(parts[0].shape[:-1] + (size * 4,), parts[0].dtype)
        for k, part in enumerate(parts):
            start = (0,) * (out.ndim - 1) + ((k ^ key) * size,)
            out = lax.dynamic_update_slice(out, part, start)
        return out

    def gathered(shard, axis_units, axis_rows, merged):
        piece = core_exchange(shard, axis_units, axis_rows)
        other = swap(piece, "zh")
        if merged:
            both = jnp.concatenate([piece, other], axis=axis_units)
            return plane_gather(both, axis_rows, plane)
        return (plane_gather(piece, axis_rows, plane), plane_gather(other, axis_rows, plane))

    qkv_full = gathered(w_qkv, 2, 1, False)
    out_full = gathered(w_out, 0, 1, True)
    up_t = jnp.transpose(w_up, (1, 2, 0))
    gate_full = gathered(up_t[0], 0, 1, True)
    upper_full = gathered(up_t[1], 0, 1, True)
    down_full = gathered(w_down, 0, 1, True)

    own_bias = lax.dynamic_slice_in_dim(b_qkv, c * (quarter // 2), quarter // 2, 1)
    qkv_bias = (own_bias, swap(lax.dynamic_slice_in_dim(b_qkv, c * (quarter // 2), quarter // 2, 1), "zh"))
    vectors = jnp.stack([gain_one, bias_one, gain_two, bias_two])
    pair = swap(vectors, "zl")
    vectors = block_order([vectors, pair, swap(vectors, "zh"), swap(pair, "zh")], zh * 2 + zl)
    gain_one, bias_one, gain_two, bias_two = (vectors[i : i + 1] for i in range(4))

    both_rows = jnp.stack([chain_ids, valid_slots])
    row_ids = jnp.where(c == zh, both_rows, swap(both_rows, "core"))
    chain_row, live_row = row_ids[0], row_ids[1]
    slot = jnp.arange(tokens, dtype=jnp.int32)
    same = chain_row[:, None] == chain_row[None, :]
    earlier = slot[None, :] < slot[:, None]
    positions = jnp.sum(jnp.where(same & earlier, 1, 0), axis=1).astype(jnp.int32)
    table = jnp.stack([chain_row, live_row, positions]).reshape(3, 4, share)

    def chunk(values, axis, j):
        o, h = j % 2, j // 2
        at = (c ^ o) * 2 + (zl ^ h)
        return lax.dynamic_slice_in_dim(values, at, 1, axis)

    table = jnp.concatenate([chunk(table, 1, j) for j in range(4)], axis=1).reshape(3, tokens)
    chain, live_int, positions = table[0], table[1], table[2]
    key_code = jnp.where(live_int > 0, chain, -1)[:, None]
    query_code = jnp.where(live_int > 0, chain, -2)[None, :]
    live = live_int[:share].astype(f32)[:, None]
    half_dim = HEAD_DIM // 2
    frequency = rope_base ** (-2.0 * jnp.arange(half_dim, dtype=f32) / HEAD_DIM)
    angles = positions.astype(f32)[:, None] * frequency[None, :]
    cosine, sine = jnp.cos(angles), jnp.sin(angles)
    cos = jnp.concatenate([cosine, cosine], axis=1)
    sin = jnp.concatenate([-sine, sine], axis=1)

    def send_rows(values, pieces):
        parts = []
        for k1, k2 in CORNERS:
            to_core, to_zl = zh ^ k1, zl ^ k2
            sent = [
                lax.dynamic_slice_in_dim(values, (to_core * 2 + (to_zl ^ h)) * share, share, 0)
                for h in range(pieces)
            ]
            sent = jnp.concatenate(sent, axis=0) if pieces > 1 else sent[0]
            parts.append(lax.ppermute(sent, TEAM, to_team(k1, k2)))
        return block_order(parts, c * 2 + zl)

    mine = send_rows(stream, 2)
    theirs = swap(mine, "core")
    stream_row = jnp.concatenate([mine[:share], theirs[:share], mine[share:], theirs[share:]], axis=0)
    stream_own = mine[:share]
    cot = send_rows(cotangent, 1)

    heads = []
    for r in (0, 1):
        q, k, v = qkv_project(stream_row, qkv_full[r], qkv_bias[r], cos, sin)
        mixed, lse = attend(q, k, v, key_code, query_code)
        heads.append((q, k, v, mixed, lse))
    mixed = jnp.concatenate([heads[0][3], heads[1][3]], axis=1)
    far = nn(mixed[2 * share :], out_full).astype(bf16)
    near = nn(mixed[: 2 * share], out_full).astype(bf16)
    branch = team_scatter(near, far)
    resid_one = deep_alpha * stream_own.astype(f32) + branch
    unit_one, inverse_one = layer_norm(resid_one)
    normed = unit_one * gain_one + bias_one

    unit = jnp.arange(units_here, dtype=jnp.int32)
    number = [((zh ^ r) * 2 + zl) * (2 * units_here) + c * units_here + unit for r in (0, 1)]
    unit_mask = (jnp.concatenate(number) < FF).astype(f32)[None, :]
    normed_half = team_gather(normed.astype(bf16))
    hidden_half, slope_half, value_half, ffn_half = [], [], [], [None, None]
    for h in (0, 1):
        gate = nt(normed_half[h], gate_full)
        upper = nt(normed_half[h], upper_full)
        value, slope = gelu_parts(gate)
        hidden_half.append((value * upper * unit_mask).astype(bf16))
        slope_half.append((slope * upper * unit_mask).astype(bf16))
        value_half.append((value * unit_mask).astype(bf16))
    for h in (1, 0):
        ffn_half[h] = nn(hidden_half[h], down_full).astype(bf16)
    ffn = team_scatter(ffn_half[0], ffn_half[1])
    resid_two = deep_alpha * normed + ffn
    unit_two, inverse_two = layer_norm(resid_two)
    output = (unit_two * gain_two + bias_two).astype(bf16)

    def return_rows(own):
        out = jnp.zeros((4, share, quarter), own.dtype)
        for k1, k2 in CORNERS:
            block = ((c ^ k1) * 2 + (zl ^ k2))
            sent = lax.dynamic_slice_in_dim(own, block * quarter, quarter, 1)
            got = lax.ppermute(sent, TEAM, from_team(k1, k2))
            out = lax.dynamic_update_slice(out, got[None], ((zh ^ k1) * 2 + (zl ^ k2), 0, 0))
        return out.reshape(tokens, quarter)

    output = return_rows(output)

    grad_output = cot.astype(f32) * live
    grad_resid_two, gain_two_part, bias_two_part = norm_backward(
        grad_output, unit_two, inverse_two, gain_two
    )
    ffn_grad_half = team_gather(grad_resid_two.astype(bf16))
    grad_gate_half, grad_upper_half, back_half = [], [], [None, None]
    for h in (0, 1):
        grad_hidden = nt(ffn_grad_half[h], down_full)
        grad_gate_half.append((grad_hidden * slope_half[h].astype(f32)).astype(bf16))
        grad_upper_half.append((grad_hidden * value_half[h].astype(f32)).astype(bf16))

    def weight_grad(piece):
        size = piece.shape[0] // 2
        total = added(piece[:size], swap(piece[size:], "zh"))
        return core_return(total.astype(bf16), 0, 1)

    ffn_grad = jnp.concatenate(ffn_grad_half, axis=0)
    hidden = jnp.concatenate(hidden_half, axis=0)
    down_piece = plane_scatter(tn(hidden, ffn_grad).astype(bf16), 1, plane)
    normed_wide = jnp.concatenate(normed_half, axis=0)
    for h in (1, 0):
        back_half[h] = (nn(grad_gate_half[h], gate_full) + nn(grad_upper_half[h], upper_full)).astype(bf16)
    up_grad = jnp.concatenate(
        [
            tn(jnp.concatenate(grad_gate_half, axis=0), normed_wide).astype(bf16),
            tn(jnp.concatenate(grad_upper_half, axis=0), normed_wide).astype(bf16),
        ],
        axis=0,
    )
    up_piece = plane_scatter(up_grad, 1, plane)
    grad_normed = deep_alpha * grad_resid_two + team_scatter(back_half[0], back_half[1])

    grad_normed = after(grad_normed, up_grad)
    grad_resid_one, gain_one_part, bias_one_part = norm_backward(
        grad_normed, unit_one, inverse_one, gain_one
    )
    branch_grad_half = team_gather(grad_resid_one.astype(bf16))
    branch_grad = jnp.concatenate(branch_grad_half, axis=0)
    grad_mixed = nt(branch_grad, out_full).astype(bf16)
    out_grad = tn(mixed, branch_grad).astype(bf16)
    out_piece = plane_scatter(out_grad, 1, plane)
    grad_mixed = after(grad_mixed, out_grad)
    grad_proj, qkv_grad, qkv_piece = [None, None], [None, None], [None, None]
    head_cols = quarter // 2
    for r in (1, 0):
        q, k, v, _, lse = heads[r]
        if r == 0:
            grad_mixed = after(grad_mixed, qkv_grad[1])
        grads = attend_back(
            q, k, v, grad_mixed[:, r * head_cols : (r + 1) * head_cols], key_code, query_code, lse, cos, sin
        )
        grad_proj[r] = jnp.concatenate(grads, axis=1)
        qkv_grad[r] = tn(stream_row, grad_proj[r]).astype(bf16)
        qkv_piece[r] = plane_scatter(qkv_grad[r], 0, plane)
    size = up_piece.shape[0] // 2
    grad_down = weight_grad(down_piece)
    grad_gate_w = weight_grad(up_piece[:size])
    grad_upper_w = weight_grad(up_piece[size:])
    grad_out = weight_grad(out_piece)
    rows_piece = added(qkv_piece[0], swap(qkv_piece[1], "zh")).astype(bf16)
    rows_piece = rows_piece.reshape(rows_piece.shape[0], 3, head_cols)
    grad_qkv = jnp.transpose(core_return(rows_piece, 2, 0), (1, 0, 2)).astype(f32)

    weight_r = [jnp.concatenate([qkv_full[r][i] for i in range(3)], axis=1) for r in (0, 1)]

    def stream_part(h):
        rows = slice(h * 2 * share, (h + 1) * 2 * share)
        return (nt(grad_proj[0][rows], weight_r[0]) + nt(grad_proj[1][rows], weight_r[1])).astype(bf16)

    far = stream_part(1)
    near = stream_part(0)
    grad_stream = (deep_alpha * grad_resid_one + team_scatter(near, far)).astype(bf16)
    grad_stream = return_rows(grad_stream)

    qkv_bias_part = jnp.zeros((3, width), f32)
    for r in (0, 1):
        part = jnp.sum(grad_proj[r].astype(f32), axis=0).reshape(3, head_cols)
        at = ((zh ^ r) * 2 + zl) * quarter + c * head_cols
        qkv_bias_part = lax.dynamic_update_slice(qkv_bias_part, part, (0, at))
    square_sums = jnp.stack(
        [
            jnp.sum(live * resid_one * resid_one),
            jnp.sum(live * branch * branch),
            jnp.sum(live * ffn * ffn),
            jnp.sum(live) * width,
        ]
    )
    norm_parts = jnp.stack([gain_one_part, bias_one_part, gain_two_part, bias_two_part])
    sums = jnp.concatenate([norm_parts, qkv_bias_part, jnp.pad(square_sums[None], ((0, 0), (0, width - 4)))])
    for axis in TEAM:
        sums = sums + swap(sums, axis)
    if square:
        for axis in plane:
            sums = sums + swap(sums, axis)
    else:
        sums = lax.psum(sums, plane)
    mine = lax.dynamic_slice_in_dim(sums[:7], (zh * 2 + zl) * quarter, quarter, 1)
    stream_stats = jnp.sqrt(sums[7, :3] / sums[7, 3])

    grad_up = jnp.stack([grad_gate_w, grad_upper_w]).astype(bf16)
    grad_up = jnp.transpose(grad_up, (2, 0, 1)).astype(f32)
    return (
        output,
        grad_stream,
        grad_qkv,
        mine[4:7],
        grad_out.astype(f32),
        mine[0],
        mine[1],
        grad_up,
        grad_down.astype(f32),
        mine[2],
        mine[3],
        stream_stats,
    )


def solution(mesh):
    wide, narrow = mesh.shape["wide"], mesh.shape["narrow"]
    square = wide == 8
    if square:
        plane, dims = ("y", "x"), (2, 2)
    else:
        plane, dims = ("plane",), (wide // 2,)
    fine = Mesh(mesh.devices.reshape(dims + (2, 2, narrow // 2)), plane + TEAM)
    w, n = plane + ("core",), ("zh", "zl")
    placed = (
        P(w, n),
        P(w),
        P(w),
        P(None, w, n),
        P(None, n),
        P(n, w),
        P(n),
        P(n),
        P(w, None, n),
        P(n, w),
        P(n),
        P(n),
        P(w, n),
    )
    return jax.shard_map(
        functools.partial(body, square),
        mesh=fine,
        in_specs=placed,
        out_specs=(
            P(w, n),
            P(w, n),
            P(None, w, n),
            P(None, n),
            P(n, w),
            P(n),
            P(n),
            P(w, None, n),
            P(n, w),
            P(n),
            P(n),
            P(),
        ),
        check_vma=False,
    )
```

```python
import functools
import math

import jax
import jax.numpy as jnp
import numpy as np
from jax import lax
from jax.experimental import pallas as pl
from jax.experimental.pallas import tpu as pltpu
from jax.sharding import Mesh
from jax.sharding import PartitionSpec as P

HEAD_DIM = 128
FF = 5461

deep_alpha = 6.928203230275509
norm_eps = 1e-05
mask_value = -1e30
rope_base = 10000.0
score_scale = 1.0 / math.sqrt(HEAD_DIM)

f32 = jnp.float32
bf16 = jnp.bfloat16
SWAP = [(0, 1), (1, 0)]


def swap(values, axis):
    return lax.ppermute(values, axis, SWAP)


def qkv_kernel(s_ref, w_ref, b_ref, cos_ref, sin_ref, q_ref, k_ref, v_ref):
    rows = s_ref[...]
    cos, sin = cos_ref[...], sin_ref[...]
    for c, out in enumerate((q_ref, k_ref, v_ref)):
        acc = jnp.dot(rows, w_ref[0, c], preferred_element_type=f32) + b_ref[c : c + 1, :]
        if c == 2:
            out[...] = acc.astype(bf16)
            continue
        for h in range(acc.shape[1] // HEAD_DIM):
            cols = slice(h * HEAD_DIM, (h + 1) * HEAD_DIM)
            head = acc[:, cols]
            turned = pltpu.roll(head, HEAD_DIM // 2, 1)
            out[:, cols] = (head * cos + turned * sin).astype(bf16)


def qkv_project(stream_row, weight, r, bias, cos, sin):
    tokens, depth = stream_row.shape
    cols = weight.shape[3]
    tile = 256
    shape = jax.ShapeDtypeStruct((tokens, cols), bf16)
    return pl.pallas_call(
        qkv_kernel,
        grid=(tokens // tile,),
        in_specs=[
            pl.BlockSpec((tile, depth), lambda i: (i, 0)),
            pl.BlockSpec((1, 3, depth, cols), lambda i: (r, 0, 0, 0)),
            pl.BlockSpec((3, cols), lambda i: (0, 0)),
            pl.BlockSpec((tile, HEAD_DIM), lambda i: (i, 0)),
            pl.BlockSpec((tile, HEAD_DIM), lambda i: (i, 0)),
        ],
        out_specs=[pl.BlockSpec((tile, cols), lambda i: (i, 0))] * 3,
        out_shape=[shape] * 3,
        name="qkv_project",
        cost_estimate=pl.CostEstimate(
            flops=2 * tokens * depth * 3 * cols,
            bytes_accessed=2 * (tokens * depth + 3 * depth * cols + 3 * tokens * cols),
            transcendentals=0,
        ),
    )(stream_row, weight, bias, cos, sin)


def allowed_of(key_code, query_code):
    return (key_code == query_code) | ((query_code < 0) & (key_code >= 0))


def attend_kernel(q_ref, k_ref, v_ref, kc_ref, qc_ref, o_ref, lse_ref):
    scores = lax.dot_general(
        k_ref[...], q_ref[...], (((1,), (1,)), ((), ())), preferred_element_type=f32
    )
    scores = jnp.where(allowed_of(kc_ref[...], qc_ref[...]), scores * score_scale, mask_value)
    top = jnp.max(scores, axis=0, keepdims=True)
    weights = jnp.exp(scores - top)
    total = jnp.sum(weights, axis=0, keepdims=True)
    mixed = lax.dot_general(
        v_ref[...], weights.astype(bf16), (((0,), (0,)), ((), ())), preferred_element_type=f32
    )
    o_ref[...] = jnp.transpose(mixed / total).astype(bf16)
    lse_ref[0] = top + jnp.log(total)


def attend(query, keys, value, key_code, query_code):
    tokens, cols = query.shape
    heads = cols // HEAD_DIM
    tile = 256
    per_q = pl.BlockSpec((tile, HEAD_DIM), lambda h, i: (i, h))
    per_head = pl.BlockSpec((tokens, HEAD_DIM), lambda h, i: (0, h))
    return pl.pallas_call(
        attend_kernel,
        grid=(heads, tokens // tile),
        in_specs=[
            per_q,
            per_head,
            per_head,
            pl.BlockSpec((tokens, 1), lambda h, i: (0, 0)),
            pl.BlockSpec((1, tile), lambda h, i: (0, i)),
        ],
        out_specs=[per_q, pl.BlockSpec((1, 1, tile), lambda h, i: (h, 0, i))],
        out_shape=[
            jax.ShapeDtypeStruct((tokens, cols), bf16),
            jax.ShapeDtypeStruct((heads, 1, tokens), f32),
        ],
        name="attend",
        cost_estimate=pl.CostEstimate(
            flops=4 * tokens * tokens * cols,
            bytes_accessed=8 * tokens * cols,
            transcendentals=heads * tokens * tokens,
        ),
    )(query, keys, value, key_code, query_code)


def attend_back_kernel(
    q_ref, k_ref, v_ref, g_ref, kc_ref, qc_ref, lse_ref, cosq_ref, sinq_ref, cosk_ref, sink_ref,
    dq_ref, dk_ref, dv_ref, dk_acc, dv_acc,
):
    step = pl.program_id(1)

    @pl.when(step == 0)
    def _():
        dk_acc[...] = jnp.zeros_like(dk_acc)
        dv_acc[...] = jnp.zeros_like(dv_acc)

    query, keys, grads = q_ref[...], k_ref[...], g_ref[...]
    nt = (((1,), (1,)), ((), ()))
    scores = lax.dot_general(keys, query, nt, preferred_element_type=f32)
    scores = jnp.where(allowed_of(kc_ref[...], qc_ref[...]), scores * score_scale, mask_value)
    probs = jnp.exp(scores - lse_ref[0])
    grad_probs = lax.dot_general(v_ref[...], grads, nt, preferred_element_type=f32)
    mean = jnp.sum(probs * grad_probs, axis=0, keepdims=True)
    grad_scores = (probs * (grad_probs - mean)).astype(bf16)
    dv_acc[...] += jnp.dot(probs.astype(bf16), grads, preferred_element_type=f32)
    dk_acc[...] += jnp.dot(grad_scores, query, preferred_element_type=f32)
    dq = jnp.transpose(
        lax.dot_general(keys, grad_scores, (((0,), (0,)), ((), ())), preferred_element_type=f32)
    )
    dq = dq * score_scale
    half = HEAD_DIM // 2
    dq_ref[...] = (dq * cosq_ref[...] - pltpu.roll(dq, half, 1) * sinq_ref[...]).astype(bf16)

    @pl.when(step == pl.num_programs(1) - 1)
    def _():
        dk = dk_acc[...] * score_scale
        dk_ref[...] = (dk * cosk_ref[...] - pltpu.roll(dk, half, 1) * sink_ref[...]).astype(bf16)
        dv_ref[...] = dv_acc[...].astype(bf16)


def attend_back(query, keys, value, grad_mixed, key_code, query_code, lse, cos, sin):
    tokens, cols = query.shape
    heads = cols // HEAD_DIM
    tile = 256
    per_q = pl.BlockSpec((tile, HEAD_DIM), lambda h, i: (i, h))
    per_head = pl.BlockSpec((tokens, HEAD_DIM), lambda h, i: (0, h))
    table_q = pl.BlockSpec((tile, HEAD_DIM), lambda h, i: (i, 0))
    table = pl.BlockSpec((tokens, HEAD_DIM), lambda h, i: (0, 0))
    return pl.pallas_call(
        attend_back_kernel,
        grid=(heads, tokens // tile),
        in_specs=[
            per_q,
            per_head,
            per_head,
            per_q,
            pl.BlockSpec((tokens, 1), lambda h, i: (0, 0)),
            pl.BlockSpec((1, tile), lambda h, i: (0, i)),
            pl.BlockSpec((1, 1, tile), lambda h, i: (h, 0, i)),
            table_q,
            table_q,
            table,
            table,
        ],
        out_specs=[per_q, per_head, per_head],
        out_shape=[jax.ShapeDtypeStruct((tokens, cols), bf16)] * 3,
        scratch_shapes=[pltpu.VMEM((tokens, HEAD_DIM), f32)] * 2,
        name="attend_back",
        cost_estimate=pl.CostEstimate(
            flops=10 * tokens * tokens * cols,
            bytes_accessed=14 * tokens * cols,
            transcendentals=heads * tokens * tokens,
        ),
    )(query, keys, value, grad_mixed, key_code, query_code, lse, cos, sin, cos, sin)


def by_core(mine, other, axis):
    c, size = lax.axis_index("core"), mine.shape[axis]
    shape = list(mine.shape)
    shape[axis] = 2 * size
    out = lax.dynamic_update_slice_in_dim(jnp.zeros(shape, mine.dtype), mine, c * size, axis)
    return lax.dynamic_update_slice_in_dim(out, other, (1 - c) * size, axis)


def halves_by_core(values, axis):
    size = values.shape[axis] // 2
    c = lax.axis_index("core")
    return (
        lax.dynamic_slice_in_dim(values, c * size, size, axis),
        lax.dynamic_slice_in_dim(values, (1 - c) * size, size, axis),
    )


def core_exchange(shard, axis_units, axis_rows):
    keep, give = halves_by_core(shard, axis_units)
    return by_core(keep, swap(give, "core"), axis_rows)


def core_return(piece, axis_units, axis_rows):
    keep, give = halves_by_core(piece, axis_rows)
    return by_core(keep, swap(give, "core"), axis_units)


def plane_gather(piece, axis, plane):
    return lax.all_gather(piece, plane, axis=axis, tiled=True)


def plane_scatter(product, axis, plane):
    return lax.psum_scatter(product, plane, scatter_dimension=axis, tiled=True)


def added(*terms):
    total = terms[0].astype(f32)
    for term in terms[1:]:
        total = total + term.astype(f32)
    return total


def after(values, *earlier):
    return lax.optimization_barrier((values, *earlier))[0]


def team_gather(own):
    core = swap(own, "core")
    chip = swap(own, "zl")
    return (
        jnp.concatenate([own, core], axis=0),
        jnp.concatenate([chip, swap(chip, "core")], axis=0),
    )


def team_scatter(near, far):
    share = far.shape[0] // 2
    far_sum = added(far[:share], swap(far[share:].astype(bf16), "core")).astype(bf16)
    from_chip = swap(far_sum, "zl")
    from_core = swap(near[share:].astype(bf16), "core")
    return added(near[:share], from_core, from_chip)


TEAM = ("core", "zh", "zl")


def team_index(c, zh, zl):
    return c * 4 + zh * 2 + zl


def to_team(k1, k2):
    return [
        (team_index(c, h, q), team_index(h ^ k1, c, q ^ k2))
        for c in (0, 1)
        for h in (0, 1)
        for q in (0, 1)
    ]


def from_team(k1, k2):
    return [(b, a) for a, b in to_team(k1, k2)]


CORNERS = [(0, 0), (0, 1), (1, 0), (1, 1)]


def first_exchange_kernel(
    stream_ref, qkv_ref, out_ref, ffn_ref, vec_ref, bias_ref,
    row_ref, qkv_full_ref, out_full_ref, gate_ref, vecs_ref, bias_far_ref,
    send, recv, local,
):
    y, x = lax.axis_index("y"), lax.axis_index("x")
    c, zh, zl = (lax.axis_index(a) for a in TEAM)
    z = zh * 2 + zl
    mine = y * 2 + x
    share = row_ref.shape[0] // 4
    quarter = stream_ref.shape[1]
    rows = qkv_ref.shape[1]
    units = out_ref.shape[0]
    to_x, to_y = {"x": 1 - x}, {"y": 1 - y}
    to_core, to_zl, to_zh = {"core": 1 - c}, {"zl": 1 - zl}, {"zh": 1 - zh}
    both_z = {"zh": 1 - zh, "zl": 1 - zl}

    barrier = pltpu.get_barrier_semaphore()

    def greet(device):
        pl.semaphore_signal(barrier, inc=1, device_id=device, device_id_type=pl.DeviceIdType.MESH)

    greet(to_x)
    greet(to_y)
    for flip in range(1, 8):
        greet({"core": c ^ (flip >> 2), "zh": zh ^ ((flip >> 1) & 1), "zl": zl ^ (flip & 1)})
    pl.semaphore_wait(barrier, 9)

    used = [0]

    def remote(src, dst, device):
        i = used[0]
        used[0] += 1
        return pltpu.make_async_remote_copy(
            src_ref=src,
            dst_ref=dst,
            send_sem=send.at[i],
            recv_sem=recv.at[i],
            device_id=device,
            device_id_type=pl.DeviceIdType.MESH,
        )

    def started(copy):
        copy.start()
        return copy

    def block(i):
        return pl.ds(pl.multiple_of(i * quarter, quarter), quarter)

    def qkv_at(r, owner, half=None):
        if half is None:
            return qkv_full_ref.at[r, :, pl.ds(pl.multiple_of(owner * rows, rows), rows), :]
        size = rows // 2
        return qkv_full_ref.at[
            r, :, pl.ds(pl.multiple_of(owner * rows + half * size, size), size), :
        ]

    def out_at(r, owner, half=None):
        if half is None:
            return out_full_ref.at[r, :, block(owner)]
        size = units // 2
        return out_full_ref.at[r, pl.ds(half * size, size), block(owner)]

    def chunk_copies(values_ref, target_ref):
        copies = []
        for k1, k2 in CORNERS:
            core_to, zl_to = zh ^ k1, zl ^ k2
            at = pl.multiple_of((core_to * 2 + zl_to) * share, share)
            copies.append(
                remote(
                    values_ref.at[pl.ds(at, share), :],
                    target_ref.at[pl.ds(0, share), block(z)],
                    {"core": core_to, "zh": c, "zl": zl_to},
                )
            )
        at = pl.multiple_of((c * 2 + zl) * share, share)
        stays = pltpu.make_async_copy(
            values_ref.at[pl.ds(at, share), :],
            target_ref.at[pl.ds(0, share), block(z)],
            local.at[2],
        )
        return copies, stays

    def start_chunks(copies, stays):
        @pl.when(c == zh)
        def _():
            stays.start()

        @pl.when(c != zh)
        def _():
            copies[0].start()

        for copy in copies[1:]:
            copy.start()

    def wait_chunks(copies, stays):
        @pl.when(c == zh)
        def _():
            stays.wait()

        @pl.when(c != zh)
        def _():
            copies[0].wait()

        for copy in copies[1:]:
            copy.wait()

    stream_copies, stream_stays = chunk_copies(stream_ref, row_ref)
    start_chunks(stream_copies, stream_stays)
    qkv_x = started(remote(qkv_ref, qkv_at(0, mine), to_x))
    qkv_y = started(remote(qkv_ref, qkv_at(0, mine), to_y))
    out_x = started(remote(out_ref, out_at(0, mine), to_x))
    out_y = started(remote(out_ref, out_at(0, mine), to_y))
    keep_qkv = pltpu.make_async_copy(qkv_ref, qkv_at(0, mine), local.at[0])
    keep_out = pltpu.make_async_copy(out_ref, out_at(0, mine), local.at[1])
    keep_qkv.start()
    keep_out.start()
    qkv_z = started(remote(qkv_ref, qkv_at(1, mine), to_zh))
    small = []
    for device in (to_zl, to_zh, both_z):
        small.append(started(remote(vec_ref, vecs_ref.at[z], device)))
    small.append(started(remote(bias_ref, bias_far_ref, to_zh)))
    vec_own = pltpu.make_async_copy(vec_ref, vecs_ref.at[z], local.at[3])
    vec_own.start()

    qkv_x.wait_recv()
    relay = [started(remote(qkv_at(0, mine ^ 1, 0), qkv_at(0, mine ^ 1, 0), to_y))]
    qkv_y.wait_recv()
    relay.append(started(remote(qkv_at(0, mine ^ 2, 1), qkv_at(0, mine ^ 2, 1), to_x)))
    wait_chunks(stream_copies, stream_stays)
    own_rows = row_ref.at[pl.ds(0, share), :]
    row_z = started(remote(own_rows, row_ref.at[pl.ds(2 * share, share), :], to_zl))
    row_c = started(remote(own_rows, row_ref.at[pl.ds(share, share), :], to_core))
    out_z = started(remote(out_ref, out_at(1, mine), to_zh))
    gate_z = started(remote(ffn_ref.at[pl.ds(0, gate_ref.shape[0]), :], gate_ref, to_zh))
    out_x.wait_recv()
    relay.append(started(remote(out_at(0, mine ^ 1, 0), out_at(0, mine ^ 1, 0), to_y)))
    out_y.wait_recv()
    relay.append(started(remote(out_at(0, mine ^ 2, 1), out_at(0, mine ^ 2, 1), to_x)))
    qkv_z.wait_recv()
    far_qkv_x = started(remote(qkv_at(1, mine), qkv_at(1, mine), to_x))
    far_qkv_y = started(remote(qkv_at(1, mine), qkv_at(1, mine), to_y))
    row_z.wait_recv()
    far_rows = row_ref.at[pl.ds(2 * share, share), :]
    row_d = started(remote(far_rows, row_ref.at[pl.ds(3 * share, share), :], to_core))
    out_z.wait_recv()
    far_out_x = started(remote(out_at(1, mine), out_at(1, mine), to_x))
    far_out_y = started(remote(out_at(1, mine), out_at(1, mine), to_y))
    far_qkv_x.wait_recv()
    relay.append(started(remote(qkv_at(1, mine ^ 1, 0), qkv_at(1, mine ^ 1, 0), to_y)))
    far_qkv_y.wait_recv()
    relay.append(started(remote(qkv_at(1, mine ^ 2, 1), qkv_at(1, mine ^ 2, 1), to_x)))
    far_out_x.wait_recv()
    relay.append(started(remote(out_at(1, mine ^ 1, 0), out_at(1, mine ^ 1, 0), to_y)))
    far_out_y.wait_recv()
    relay.append(started(remote(out_at(1, mine ^ 2, 1), out_at(1, mine ^ 2, 1), to_x)))

    for copy in (row_c, row_d, gate_z, *small, *relay):
        copy.wait_recv()
    for copy in (
        qkv_x, qkv_y, out_x, out_y, qkv_z, row_z, row_c, out_z, gate_z, row_d,
        far_qkv_x, far_qkv_y, far_out_x, far_out_y, *small, *relay,
    ):
        copy.wait_send()
    for copy in (keep_qkv, keep_out, vec_own):
        copy.wait()


def first_exchange(stream, qkv, out, ffn, vectors, bias):
    tokens, quarter = stream.shape
    width = quarter * 4
    hbm = pl.BlockSpec(memory_space=pl.ANY)
    copies = 40
    return pl.pallas_call(
        first_exchange_kernel,
        in_specs=[hbm] * 6,
        out_specs=[hbm] * 6,
        out_shape=[
            jax.ShapeDtypeStruct((tokens, width), bf16),
            jax.ShapeDtypeStruct((2, 3, width, qkv.shape[2]), bf16),
            jax.ShapeDtypeStruct((2, out.shape[0], width), bf16),
            jax.ShapeDtypeStruct((ffn.shape[0] // 3, ffn.shape[1]), bf16),
            jax.ShapeDtypeStruct((4,) + vectors.shape, f32),
            jax.ShapeDtypeStruct(bias.shape, f32),
        ],
        scratch_shapes=[
            pltpu.SemaphoreType.DMA((copies,)),
            pltpu.SemaphoreType.DMA((copies,)),
            pltpu.SemaphoreType.DMA((4,)),
        ],
        compiler_params=pltpu.CompilerParams(collective_id=1, has_side_effects=True),
        name="first_exchange",
    )(stream, qkv, out, ffn, vectors, bias)


def layer_norm(resid):
    centred = resid - jnp.mean(resid, axis=1, keepdims=True)
    inverse = lax.rsqrt(jnp.mean(centred * centred, axis=1, keepdims=True) + norm_eps)
    return centred * inverse, inverse


def norm_backward(grad_in, unit, inverse, gain):
    grad_unit = grad_in * gain
    first = jnp.mean(grad_unit, axis=1, keepdims=True)
    second = jnp.mean(grad_unit * unit, axis=1, keepdims=True)
    grad_resid = inverse * (grad_unit - first - unit * second)
    return grad_resid, jnp.sum(grad_in * unit, axis=0), jnp.sum(grad_in, axis=0)


def gelu_parts(gate):
    root = math.sqrt(2.0 / math.pi)
    inner = jnp.tanh(root * (gate + 0.044715 * gate * gate * gate))
    half = 0.5 * (1.0 + inner)
    slope = half + 0.5 * gate * (1.0 - inner * inner) * root * (1.0 + 3 * 0.044715 * gate * gate)
    return gate * half, slope


def nt(a, b):
    return lax.dot_general(a, b, (((1,), (1,)), ((), ())), preferred_element_type=f32)


def nn(a, b):
    return jnp.dot(a, b, preferred_element_type=f32)


def tn(a, b):
    return lax.dot_general(a, b, (((0,), (0,)), ((), ())), preferred_element_type=f32)


def body(
    square,
    stream,
    chain_ids,
    valid_slots,
    w_qkv,
    b_qkv,
    w_out,
    gain_one,
    bias_one,
    w_up,
    w_down,
    gain_two,
    bias_two,
    cotangent,
):
    c, zh, zl = (lax.axis_index(a) for a in TEAM)
    tokens, quarter = stream.shape
    width = quarter * 4
    share = tokens // 4
    plane = ("y", "x") if square else ("plane",)
    units_here = w_down.shape[0] // 2

    def block_order(parts, key):
        size = parts[0].shape[-1]
        out = jnp.zeros(parts[0].shape[:-1] + (size * 4,), parts[0].dtype)
        for k, part in enumerate(parts):
            start = (0,) * (out.ndim - 1) + ((k ^ key) * size,)
            out = lax.dynamic_update_slice(out, part, start)
        return out

    def send_rows(values, pieces):
        parts = []
        for k1, k2 in CORNERS:
            to_core, to_zl = zh ^ k1, zl ^ k2
            sent = [
                lax.dynamic_slice_in_dim(values, (to_core * 2 + (to_zl ^ h)) * share, share, 0)
                for h in range(pieces)
            ]
            sent = jnp.concatenate(sent, axis=0) if pieces > 1 else sent[0]
            parts.append(lax.ppermute(sent, TEAM, to_team(k1, k2)))
        return block_order(parts, c * 2 + zl)

    head_cols = quarter // 2
    qkv_piece = core_exchange(w_qkv, 2, 1)
    out_piece = core_exchange(w_out, 0, 1)
    up_t = jnp.transpose(w_up, (1, 2, 0))
    kept, given = zip(halves_by_core(up_t[0], 0), halves_by_core(up_t[1], 0), halves_by_core(w_down, 0))
    ffn_piece = by_core(jnp.concatenate(kept, axis=0), swap(jnp.concatenate(given, axis=0), "core"), 1)
    vectors = jnp.stack([gain_one, bias_one, gain_two, bias_two])
    own_bias = lax.dynamic_slice_in_dim(b_qkv, c * head_cols, head_cols, 1)
    third = units_here
    if square:
        stream_row, qkv_full, out_full, gate_far, vectors, far_bias = first_exchange(
            stream,
            qkv_piece,
            out_piece,
            ffn_piece,
            jnp.pad(vectors, ((0, 4), (0, 0))),
            jnp.pad(own_bias, ((0, 5), (0, 0))),
        )
        qkv_bias = (own_bias, far_bias[:3])
        vectors = jnp.transpose(vectors, (1, 0, 2)).reshape(8, width)
        out_full = out_full.reshape(2 * head_cols, width)
        stream_own = stream_row[:share]
        upper_far = swap(after(ffn_piece, gate_far)[third : 2 * third], "zh")
        down_far = swap(after(ffn_piece, gate_far)[2 * third :], "zh")
        ffn_far = jnp.concatenate([gate_far, upper_far, down_far], axis=0)
    else:
        both = jnp.concatenate([out_piece, swap(out_piece, "zh")], axis=0)
        out_full = plane_gather(both, 1, plane)
        qkv_full = jnp.stack([plane_gather(qkv_piece, 1, plane), plane_gather(swap(qkv_piece, "zh"), 1, plane)])
        ffn_far = swap(ffn_piece, "zh")
        qkv_bias = (own_bias, swap(own_bias, "zh"))
        pair = swap(vectors, "zl")
        vectors = block_order([vectors, pair, swap(vectors, "zh"), swap(pair, "zh")], zh * 2 + zl)
        mine = send_rows(stream, 2)
        theirs = swap(mine, "core")
        stream_row = jnp.concatenate([mine[:share], theirs[:share], mine[share:], theirs[share:]], axis=0)
        stream_own = mine[:share]
    ffn_near = plane_gather(ffn_piece, 1, plane)
    gain_one, bias_one, gain_two, bias_two = (vectors[i : i + 1] for i in range(4))

    both_rows = jnp.stack([chain_ids, valid_slots])
    row_ids = jnp.where(c == zh, both_rows, swap(both_rows, "core"))
    chain_row, live_row = row_ids[0], row_ids[1]
    slot = jnp.arange(tokens, dtype=jnp.int32)
    same = chain_row[:, None] == chain_row[None, :]
    earlier = slot[None, :] < slot[:, None]
    positions = jnp.sum(jnp.where(same & earlier, 1, 0), axis=1).astype(jnp.int32)
    table = jnp.stack([chain_row, live_row, positions]).reshape(3, 4, share)

    def chunk(values, axis, j):
        o, h = j % 2, j // 2
        at = (c ^ o) * 2 + (zl ^ h)
        return lax.dynamic_slice_in_dim(values, at, 1, axis)

    table = jnp.concatenate([chunk(table, 1, j) for j in range(4)], axis=1).reshape(3, tokens)
    chain, live_int, positions = table[0], table[1], table[2]
    key_code = jnp.where(live_int > 0, chain, -1)[:, None]
    query_code = jnp.where(live_int > 0, chain, -2)[None, :]
    live = live_int[:share].astype(f32)[:, None]
    half_dim = HEAD_DIM // 2
    frequency = rope_base ** (-2.0 * jnp.arange(half_dim, dtype=f32) / HEAD_DIM)
    angles = positions.astype(f32)[:, None] * frequency[None, :]
    cosine, sine = jnp.cos(angles), jnp.sin(angles)
    cos = jnp.concatenate([cosine, cosine], axis=1)
    sin = jnp.concatenate([-sine, sine], axis=1)

    heads = []
    for r in (0, 1):
        q, k, v = qkv_project(stream_row, qkv_full, r, qkv_bias[r], cos, sin)
        mixed, lse = attend(q, k, v, key_code, query_code)
        heads.append((q, k, v, mixed, lse))
    ffn_far = plane_gather(after(ffn_far, heads[0][3]), 1, plane)
    gate_full = jnp.concatenate([ffn_near[:third], ffn_far[:third]], axis=0)
    upper_full = jnp.concatenate([ffn_near[third : 2 * third], ffn_far[third : 2 * third]], axis=0)
    down_full = jnp.concatenate([ffn_near[2 * third :], ffn_far[2 * third :]], axis=0)
    mixed = jnp.concatenate([heads[0][3], heads[1][3]], axis=1)
    far = nn(mixed[2 * share :], out_full).astype(bf16)
    near = nn(mixed[: 2 * share], out_full).astype(bf16)
    branch = team_scatter(near, far)
    resid_one = deep_alpha * stream_own.astype(f32) + branch
    unit_one, inverse_one = layer_norm(resid_one)
    normed = unit_one * gain_one + bias_one

    unit = jnp.arange(units_here, dtype=jnp.int32)
    number = [((zh ^ r) * 2 + zl) * (2 * units_here) + c * units_here + unit for r in (0, 1)]
    unit_mask = (jnp.concatenate(number) < FF).astype(f32)[None, :]
    normed_half = team_gather(normed.astype(bf16))
    cot = send_rows(after(cotangent, normed_half[1]), 1)
    hidden_half, slope_half, value_half, ffn_half = [], [], [], [None, None]
    for h in (0, 1):
        gate = nt(normed_half[h], gate_full)
        upper = nt(normed_half[h], upper_full)
        value, slope = gelu_parts(gate)
        hidden_half.append((value * upper * unit_mask).astype(bf16))
        slope_half.append((slope * upper * unit_mask).astype(bf16))
        value_half.append((value * unit_mask).astype(bf16))
    for h in (1, 0):
        ffn_half[h] = nn(hidden_half[h], down_full).astype(bf16)
    ffn = team_scatter(ffn_half[0], ffn_half[1])
    resid_two = deep_alpha * normed + ffn
    unit_two, inverse_two = layer_norm(resid_two)
    output = (unit_two * gain_two + bias_two).astype(bf16)

    def return_rows(own):
        out = jnp.zeros((4, share, quarter), own.dtype)
        for k1, k2 in CORNERS:
            block = ((c ^ k1) * 2 + (zl ^ k2))
            sent = lax.dynamic_slice_in_dim(own, block * quarter, quarter, 1)
            got = lax.ppermute(sent, TEAM, from_team(k1, k2))
            out = lax.dynamic_update_slice(out, got[None], ((zh ^ k1) * 2 + (zl ^ k2), 0, 0))
        return out.reshape(tokens, quarter)

    output = return_rows(output)

    grad_output = cot.astype(f32) * live
    grad_resid_two, gain_two_part, bias_two_part = norm_backward(
        grad_output, unit_two, inverse_two, gain_two
    )
    ffn_grad_half = team_gather(grad_resid_two.astype(bf16))
    grad_units_half, back_half = [], [None, None]
    which = lax.broadcasted_iota(jnp.int32, (2, 1, 1), 0)
    for h in (0, 1):
        grad_hidden = nt(ffn_grad_half[h], down_full)
        factor = jnp.where(which == 0, slope_half[h][None], value_half[h][None])
        grad_units_half.append((grad_hidden[None] * factor.astype(f32)).astype(bf16))

    def weight_grad(own, other):
        return core_return(added(own, other).astype(bf16), 0, 1)

    ffn_grad = jnp.concatenate(ffn_grad_half, axis=0)
    hidden = jnp.concatenate(hidden_half, axis=0)
    down_grad = tn(hidden, ffn_grad).astype(bf16)
    down_piece = plane_scatter(down_grad, 1, plane)
    normed_wide = jnp.concatenate(normed_half, axis=0)
    grad_units_half[1] = after(grad_units_half[1], down_grad)
    for h in (1, 0):
        grad_units = grad_units_half[h]
        back_half[h] = (nn(grad_units[0], gate_full) + nn(grad_units[1], upper_full)).astype(bf16)
    up_grad = lax.dot_general(
        jnp.concatenate(grad_units_half, axis=1), normed_wide, (((1,), (0,)), ((), ())), preferred_element_type=f32
    )
    up_grad = up_grad.astype(bf16).reshape(-1, width)
    grad_normed = deep_alpha * grad_resid_two + team_scatter(back_half[0], back_half[1])

    grad_normed = after(grad_normed, up_grad)
    grad_resid_one, gain_one_part, bias_one_part = norm_backward(
        grad_normed, unit_one, inverse_one, gain_one
    )
    branch_grad_half = team_gather(grad_resid_one.astype(bf16))
    branch_grad = jnp.concatenate(branch_grad_half, axis=0)
    up_piece = plane_scatter(after(up_grad, branch_grad), 1, plane).reshape(2, 2, units_here, -1)
    grad_mixed = nt(branch_grad, out_full).astype(bf16)
    out_grad = tn(mixed, branch_grad).astype(bf16)
    grad_mixed = after(grad_mixed, out_grad, down_piece)
    grad_proj, qkv_grad, qkv_sum = [None, None], [None, None], [None, None]
    for r in (1, 0):
        q, k, v, _, lse = heads[r]
        if r == 0:
            down_swapped = swap(down_piece[units_here:], "zh")
            grad_mixed = after(grad_mixed, qkv_grad[1])
        grads = attend_back(
            q, k, v, grad_mixed[:, r * head_cols : (r + 1) * head_cols], key_code, query_code, lse, cos, sin
        )
        grad_proj[r] = jnp.concatenate(grads, axis=1)
        qkv_grad[r] = tn(stream_row, grad_proj[r]).astype(bf16)
    grad_down = weight_grad(down_piece[:units_here], down_swapped)
    up_swapped = swap(up_piece[:, 1], "zh")
    out_sum = plane_scatter(after(out_grad, up_piece, grad_proj[0]), 1, plane)
    for r in (1, 0):
        qkv_sum[r] = plane_scatter(after(qkv_grad[r], up_piece, grad_proj[0]), 0, plane)
    grad_gate_w = weight_grad(up_piece[0, 0], up_swapped[0])
    grad_upper_w = weight_grad(up_piece[1, 0], up_swapped[1])
    grad_out = weight_grad(out_sum[:head_cols], swap(out_sum[head_cols:], "zh"))
    rows_piece = added(qkv_sum[0], swap(qkv_sum[1], "zh")).astype(bf16)
    rows_piece = rows_piece.reshape(rows_piece.shape[0], 3, head_cols)
    grad_qkv = jnp.transpose(core_return(rows_piece, 2, 0), (1, 0, 2)).astype(f32)

    weight_r = [jnp.concatenate([qkv_full[r][i] for i in range(3)], axis=1) for r in (0, 1)]

    def stream_part(h):
        rows = slice(h * 2 * share, (h + 1) * 2 * share)
        return (nt(grad_proj[0][rows], weight_r[0]) + nt(grad_proj[1][rows], weight_r[1])).astype(bf16)

    far = stream_part(1)
    near = stream_part(0)
    grad_stream = (deep_alpha * grad_resid_one + team_scatter(near, far)).astype(bf16)
    grad_stream = return_rows(after(grad_stream, up_swapped, down_swapped))

    qkv_bias_part = jnp.zeros((3, width), f32)
    for r in (0, 1):
        part = jnp.sum(grad_proj[r].astype(f32), axis=0).reshape(3, head_cols)
        at = ((zh ^ r) * 2 + zl) * quarter + c * head_cols
        qkv_bias_part = lax.dynamic_update_slice(qkv_bias_part, part, (0, at))
    square_sums = jnp.stack(
        [
            jnp.sum(live * resid_one * resid_one),
            jnp.sum(live * branch * branch),
            jnp.sum(live * ffn * ffn),
            jnp.sum(live) * width,
        ]
    )
    norm_parts = jnp.stack([gain_one_part, bias_one_part, gain_two_part, bias_two_part])
    sums = jnp.concatenate([norm_parts, qkv_bias_part, jnp.pad(square_sums[None], ((0, 0), (0, width - 4)))])
    for axis in TEAM:
        sums = sums + swap(sums, axis)
    if square:
        for axis in plane:
            sums = sums + swap(sums, axis)
    else:
        sums = lax.psum(sums, plane)
    mine = lax.dynamic_slice_in_dim(sums[:7], (zh * 2 + zl) * quarter, quarter, 1)
    stream_stats = jnp.sqrt(sums[7, :3] / sums[7, 3])

    grad_up = jnp.stack([grad_gate_w, grad_upper_w]).astype(bf16)
    grad_up = jnp.transpose(grad_up, (2, 0, 1)).astype(f32)
    return (
        output,
        grad_stream,
        grad_qkv,
        mine[4:7],
        grad_out.astype(f32),
        mine[0],
        mine[1],
        grad_up,
        grad_down.astype(f32),
        mine[2],
        mine[3],
        stream_stats,
    )


def solution(mesh):
    wide, narrow = mesh.shape["wide"], mesh.shape["narrow"]
    square = wide == 8
    if square:
        plane, dims = ("y", "x"), (2, 2)
    else:
        plane, dims = ("plane",), (wide // 2,)
    fine = Mesh(mesh.devices.reshape(dims + (2, 2, narrow // 2)), plane + TEAM)
    w, n = plane + ("core",), ("zh", "zl")
    placed = (
        P(w, n),
        P(w),
        P(w),
        P(None, w, n),
        P(None, n),
        P(n, w),
        P(n),
        P(n),
        P(w, None, n),
        P(n, w),
        P(n),
        P(n),
        P(w, n),
    )
    return jax.shard_map(
        functools.partial(body, square),
        mesh=fine,
        in_specs=placed,
        out_specs=(
            P(w, n),
            P(w, n),
            P(None, w, n),
            P(None, n),
            P(n, w),
            P(n),
            P(n),
            P(w, None, n),
            P(n, w),
            P(n),
            P(n),
            P(),
        ),
        check_vma=False,
    )
```

```python
import functools
import math

import jax
import jax.numpy as jnp
import numpy as np
from jax import lax
from jax.experimental import pallas as pl
from jax.experimental.pallas import tpu as pltpu
from jax.sharding import Mesh
from jax.sharding import PartitionSpec as P

HEAD_DIM = 128
FF = 5461

deep_alpha = 6.928203230275509
norm_eps = 1e-05
mask_value = -1e30
rope_base = 10000.0
score_scale = 1.0 / math.sqrt(HEAD_DIM)

f32 = jnp.float32
bf16 = jnp.bfloat16
SWAP = [(0, 1), (1, 0)]


def swap(values, axis):
    return lax.ppermute(values, axis, SWAP)


def qkv_kernel(s_ref, w_ref, b_ref, cos_ref, sin_ref, q_ref, k_ref, v_ref):
    rows = s_ref[...]
    cos, sin = cos_ref[...], sin_ref[...]
    for c, out in enumerate((q_ref, k_ref, v_ref)):
        acc = jnp.dot(rows, w_ref[0, c], preferred_element_type=f32) + b_ref[c : c + 1, :]
        if c == 2:
            out[...] = acc.astype(bf16)
            continue
        for h in range(acc.shape[1] // HEAD_DIM):
            cols = slice(h * HEAD_DIM, (h + 1) * HEAD_DIM)
            head = acc[:, cols]
            turned = pltpu.roll(head, HEAD_DIM // 2, 1)
            out[:, cols] = (head * cos + turned * sin).astype(bf16)


def qkv_project(stream_row, weight, r, bias, cos, sin):
    tokens, depth = stream_row.shape
    cols = weight.shape[3]
    tile = 256
    shape = jax.ShapeDtypeStruct((tokens, cols), bf16)
    return pl.pallas_call(
        qkv_kernel,
        grid=(tokens // tile,),
        in_specs=[
            pl.BlockSpec((tile, depth), lambda i: (i, 0)),
            pl.BlockSpec((1, 3, depth, cols), lambda i: (r, 0, 0, 0)),
            pl.BlockSpec((3, cols), lambda i: (0, 0)),
            pl.BlockSpec((tile, HEAD_DIM), lambda i: (i, 0)),
            pl.BlockSpec((tile, HEAD_DIM), lambda i: (i, 0)),
        ],
        out_specs=[pl.BlockSpec((tile, cols), lambda i: (i, 0))] * 3,
        out_shape=[shape] * 3,
        name="qkv_project",
        cost_estimate=pl.CostEstimate(
            flops=2 * tokens * depth * 3 * cols,
            bytes_accessed=2 * (tokens * depth + 3 * depth * cols + 3 * tokens * cols),
            transcendentals=0,
        ),
    )(stream_row, weight, bias, cos, sin)


def allowed_of(key_code, query_code):
    return (key_code == query_code) | ((query_code < 0) & (key_code >= 0))


def attend_kernel(q_ref, k_ref, v_ref, kc_ref, qc_ref, o_ref, lse_ref):
    scores = lax.dot_general(
        k_ref[...], q_ref[...], (((1,), (1,)), ((), ())), preferred_element_type=f32
    )
    scores = jnp.where(allowed_of(kc_ref[...], qc_ref[...]), scores * score_scale, mask_value)
    top = jnp.max(scores, axis=0, keepdims=True)
    weights = jnp.exp(scores - top)
    total = jnp.sum(weights, axis=0, keepdims=True)
    mixed = lax.dot_general(
        v_ref[...], weights.astype(bf16), (((0,), (0,)), ((), ())), preferred_element_type=f32
    )
    o_ref[...] = jnp.transpose(mixed / total).astype(bf16)
    lse_ref[0] = top + jnp.log(total)


def attend(query, keys, value, key_code, query_code):
    tokens, cols = query.shape
    heads = cols // HEAD_DIM
    tile = 256
    per_q = pl.BlockSpec((tile, HEAD_DIM), lambda h, i: (i, h))
    per_head = pl.BlockSpec((tokens, HEAD_DIM), lambda h, i: (0, h))
    return pl.pallas_call(
        attend_kernel,
        grid=(heads, tokens // tile),
        in_specs=[
            per_q,
            per_head,
            per_head,
            pl.BlockSpec((tokens, 1), lambda h, i: (0, 0)),
            pl.BlockSpec((1, tile), lambda h, i: (0, i)),
        ],
        out_specs=[per_q, pl.BlockSpec((1, 1, tile), lambda h, i: (h, 0, i))],
        out_shape=[
            jax.ShapeDtypeStruct((tokens, cols), bf16),
            jax.ShapeDtypeStruct((heads, 1, tokens), f32),
        ],
        name="attend",
        cost_estimate=pl.CostEstimate(
            flops=4 * tokens * tokens * cols,
            bytes_accessed=8 * tokens * cols,
            transcendentals=heads * tokens * tokens,
        ),
    )(query, keys, value, key_code, query_code)


def attend_back_kernel(
    q_ref, k_ref, v_ref, g_ref, kc_ref, qc_ref, lse_ref, cosq_ref, sinq_ref, cosk_ref, sink_ref,
    dq_ref, dk_ref, dv_ref, dk_acc, dv_acc,
):
    step = pl.program_id(1)

    @pl.when(step == 0)
    def _():
        dk_acc[...] = jnp.zeros_like(dk_acc)
        dv_acc[...] = jnp.zeros_like(dv_acc)

    query, keys, grads = q_ref[...], k_ref[...], g_ref[...]
    nt = (((1,), (1,)), ((), ()))
    scores = lax.dot_general(keys, query, nt, preferred_element_type=f32)
    scores = jnp.where(allowed_of(kc_ref[...], qc_ref[...]), scores * score_scale, mask_value)
    probs = jnp.exp(scores - lse_ref[0])
    grad_probs = lax.dot_general(v_ref[...], grads, nt, preferred_element_type=f32)
    mean = jnp.sum(probs * grad_probs, axis=0, keepdims=True)
    grad_scores = (probs * (grad_probs - mean)).astype(bf16)
    dv_acc[...] += jnp.dot(probs.astype(bf16), grads, preferred_element_type=f32)
    dk_acc[...] += jnp.dot(grad_scores, query, preferred_element_type=f32)
    dq = jnp.transpose(
        lax.dot_general(keys, grad_scores, (((0,), (0,)), ((), ())), preferred_element_type=f32)
    )
    dq = dq * score_scale
    half = HEAD_DIM // 2
    dq_ref[...] = (dq * cosq_ref[...] - pltpu.roll(dq, half, 1) * sinq_ref[...]).astype(bf16)

    @pl.when(step == pl.num_programs(1) - 1)
    def _():
        dk = dk_acc[...] * score_scale
        dk_ref[...] = (dk * cosk_ref[...] - pltpu.roll(dk, half, 1) * sink_ref[...]).astype(bf16)
        dv_ref[...] = dv_acc[...].astype(bf16)


def attend_back(query, keys, value, grad_mixed, key_code, query_code, lse, cos, sin):
    tokens, cols = query.shape
    heads = cols // HEAD_DIM
    tile = 256
    per_q = pl.BlockSpec((tile, HEAD_DIM), lambda h, i: (i, h))
    per_head = pl.BlockSpec((tokens, HEAD_DIM), lambda h, i: (0, h))
    table_q = pl.BlockSpec((tile, HEAD_DIM), lambda h, i: (i, 0))
    table = pl.BlockSpec((tokens, HEAD_DIM), lambda h, i: (0, 0))
    return pl.pallas_call(
        attend_back_kernel,
        grid=(heads, tokens // tile),
        in_specs=[
            per_q,
            per_head,
            per_head,
            per_q,
            pl.BlockSpec((tokens, 1), lambda h, i: (0, 0)),
            pl.BlockSpec((1, tile), lambda h, i: (0, i)),
            pl.BlockSpec((1, 1, tile), lambda h, i: (h, 0, i)),
            table_q,
            table_q,
            table,
            table,
        ],
        out_specs=[per_q, per_head, per_head],
        out_shape=[jax.ShapeDtypeStruct((tokens, cols), bf16)] * 3,
        scratch_shapes=[pltpu.VMEM((tokens, HEAD_DIM), f32)] * 2,
        name="attend_back",
        cost_estimate=pl.CostEstimate(
            flops=10 * tokens * tokens * cols,
            bytes_accessed=14 * tokens * cols,
            transcendentals=heads * tokens * tokens,
        ),
    )(query, keys, value, grad_mixed, key_code, query_code, lse, cos, sin, cos, sin)


def by_core(mine, other, axis):
    c, size = lax.axis_index("core"), mine.shape[axis]
    shape = list(mine.shape)
    shape[axis] = 2 * size
    out = lax.dynamic_update_slice_in_dim(jnp.zeros(shape, mine.dtype), mine, c * size, axis)
    return lax.dynamic_update_slice_in_dim(out, other, (1 - c) * size, axis)


def halves_by_core(values, axis):
    size = values.shape[axis] // 2
    c = lax.axis_index("core")
    return (
        lax.dynamic_slice_in_dim(values, c * size, size, axis),
        lax.dynamic_slice_in_dim(values, (1 - c) * size, size, axis),
    )


def core_exchange(shard, axis_units, axis_rows):
    keep, give = halves_by_core(shard, axis_units)
    return by_core(keep, swap(give, "core"), axis_rows)


def core_return(piece, axis_units, axis_rows):
    keep, give = halves_by_core(piece, axis_rows)
    return by_core(keep, swap(give, "core"), axis_units)


def plane_gather(piece, axis, plane):
    return lax.all_gather(piece, plane, axis=axis, tiled=True)


def plane_scatter(product, axis, plane):
    return lax.psum_scatter(product, plane, scatter_dimension=axis, tiled=True)


def added(*terms):
    total = terms[0].astype(f32)
    for term in terms[1:]:
        total = total + term.astype(f32)
    return total


def after(values, *earlier):
    return lax.optimization_barrier((values, *earlier))[0]


def team_gather(own):
    core = swap(own, "core")
    chip = swap(own, "zl")
    return (
        jnp.concatenate([own, core], axis=0),
        jnp.concatenate([chip, swap(chip, "core")], axis=0),
    )


def chip_sum(far):
    share = far.shape[0] // 2
    return added(far[:share], swap(far[share:].astype(bf16), "core")).astype(bf16)


def team_scatter(near, far_sum):
    share = far_sum.shape[0]
    from_chip = swap(far_sum, "zl")
    from_core = swap(near[share:].astype(bf16), "core")
    return added(near[:share], from_core, from_chip)


TEAM = ("core", "zh", "zl")


def team_index(c, zh, zl):
    return c * 4 + zh * 2 + zl


def to_team(k1, k2):
    return [
        (team_index(c, h, q), team_index(h ^ k1, c, q ^ k2))
        for c in (0, 1)
        for h in (0, 1)
        for q in (0, 1)
    ]


def from_team(k1, k2):
    return [(b, a) for a, b in to_team(k1, k2)]


CORNERS = [(0, 0), (0, 1), (1, 0), (1, 1)]


def first_exchange_kernel(
    stream_ref, qkv_ref, out_ref, ffn_ref, vec_ref, bias_ref,
    row_ref, qkv_full_ref, out_full_ref, ffn_full_ref, gate_ref, vecs_ref, bias_far_ref,
    send, recv, local,
):
    y, x = lax.axis_index("y"), lax.axis_index("x")
    c, zh, zl = (lax.axis_index(a) for a in TEAM)
    z = zh * 2 + zl
    mine = y * 2 + x
    share = row_ref.shape[0] // 4
    quarter = stream_ref.shape[1]
    rows = qkv_ref.shape[1]
    units = out_ref.shape[0]
    to_x, to_y = {"x": 1 - x}, {"y": 1 - y}
    to_core, to_zl, to_zh = {"core": 1 - c}, {"zl": 1 - zl}, {"zh": 1 - zh}
    both_z = {"zh": 1 - zh, "zl": 1 - zl}

    barrier = pltpu.get_barrier_semaphore()

    def greet(device):
        pl.semaphore_signal(barrier, inc=1, device_id=device, device_id_type=pl.DeviceIdType.MESH)

    greet(to_x)
    greet(to_y)
    for flip in range(1, 8):
        greet({"core": c ^ (flip >> 2), "zh": zh ^ ((flip >> 1) & 1), "zl": zl ^ (flip & 1)})
    pl.semaphore_wait(barrier, 9)

    used = [0]

    def remote(src, dst, device):
        i = used[0]
        used[0] += 1
        return pltpu.make_async_remote_copy(
            src_ref=src,
            dst_ref=dst,
            send_sem=send.at[i],
            recv_sem=recv.at[i],
            device_id=device,
            device_id_type=pl.DeviceIdType.MESH,
        )

    def started(copy):
        copy.start()
        return copy

    def block(i):
        return pl.ds(pl.multiple_of(i * quarter, quarter), quarter)

    def qkv_at(r, owner, half=None):
        if half is None:
            return qkv_full_ref.at[r, :, pl.ds(pl.multiple_of(owner * rows, rows), rows), :]
        size = rows // 2
        return qkv_full_ref.at[
            r, :, pl.ds(pl.multiple_of(owner * rows + half * size, size), size), :
        ]

    def out_at(r, owner, half=None):
        if half is None:
            return out_full_ref.at[r, :, block(owner)]
        size = units // 2
        return out_full_ref.at[r, pl.ds(half * size, size), block(owner)]

    def ffn_at(owner, half=None):
        if half is None:
            return ffn_full_ref.at[:, block(owner)]
        size = ffn_ref.shape[0] // 2
        return ffn_full_ref.at[pl.ds(half * size, size), block(owner)]

    def chunk_copies(values_ref, target_ref):
        copies = []
        for k1, k2 in CORNERS:
            core_to, zl_to = zh ^ k1, zl ^ k2
            at = pl.multiple_of((core_to * 2 + zl_to) * share, share)
            copies.append(
                remote(
                    values_ref.at[pl.ds(at, share), :],
                    target_ref.at[pl.ds(0, share), block(z)],
                    {"core": core_to, "zh": c, "zl": zl_to},
                )
            )
        at = pl.multiple_of((c * 2 + zl) * share, share)
        stays = pltpu.make_async_copy(
            values_ref.at[pl.ds(at, share), :],
            target_ref.at[pl.ds(0, share), block(z)],
            local.at[2],
        )
        return copies, stays

    def start_chunks(copies, stays):
        @pl.when(c == zh)
        def _():
            stays.start()

        @pl.when(c != zh)
        def _():
            copies[0].start()

        for copy in copies[1:]:
            copy.start()

    def wait_chunks(copies, stays):
        @pl.when(c == zh)
        def _():
            stays.wait()

        @pl.when(c != zh)
        def _():
            copies[0].wait()

        for copy in copies[1:]:
            copy.wait()

    stream_copies, stream_stays = chunk_copies(stream_ref, row_ref)
    start_chunks(stream_copies, stream_stays)
    qkv_x = started(remote(qkv_ref, qkv_at(0, mine), to_x))
    qkv_y = started(remote(qkv_ref, qkv_at(0, mine), to_y))
    out_x = started(remote(out_ref, out_at(0, mine), to_x))
    out_y = started(remote(out_ref, out_at(0, mine), to_y))
    keep_qkv = pltpu.make_async_copy(qkv_ref, qkv_at(0, mine), local.at[0])
    keep_out = pltpu.make_async_copy(out_ref, out_at(0, mine), local.at[1])
    keep_ffn = pltpu.make_async_copy(ffn_ref, ffn_at(mine), local.at[4])
    keep_qkv.start()
    keep_out.start()
    keep_ffn.start()
    ffn_x = started(remote(ffn_ref, ffn_at(mine), to_x))
    ffn_y = started(remote(ffn_ref, ffn_at(mine), to_y))
    qkv_z = started(remote(qkv_ref, qkv_at(1, mine), to_zh))
    small = []
    for device in (to_zl, to_zh, both_z):
        small.append(started(remote(vec_ref, vecs_ref.at[z], device)))
    small.append(started(remote(bias_ref, bias_far_ref, to_zh)))
    vec_own = pltpu.make_async_copy(vec_ref, vecs_ref.at[z], local.at[3])
    vec_own.start()

    qkv_x.wait_recv()
    relay = [started(remote(qkv_at(0, mine ^ 1, 0), qkv_at(0, mine ^ 1, 0), to_y))]
    qkv_y.wait_recv()
    relay.append(started(remote(qkv_at(0, mine ^ 2, 1), qkv_at(0, mine ^ 2, 1), to_x)))
    wait_chunks(stream_copies, stream_stays)
    own_rows = row_ref.at[pl.ds(0, share), :]
    row_z = started(remote(own_rows, row_ref.at[pl.ds(2 * share, share), :], to_zl))
    row_c = started(remote(own_rows, row_ref.at[pl.ds(share, share), :], to_core))
    out_z = started(remote(out_ref, out_at(1, mine), to_zh))
    gate_z = started(remote(ffn_ref.at[pl.ds(0, gate_ref.shape[0]), :], gate_ref, to_zh))
    out_x.wait_recv()
    relay.append(started(remote(out_at(0, mine ^ 1, 0), out_at(0, mine ^ 1, 0), to_y)))
    out_y.wait_recv()
    relay.append(started(remote(out_at(0, mine ^ 2, 1), out_at(0, mine ^ 2, 1), to_x)))
    qkv_z.wait_recv()
    far_qkv_x = started(remote(qkv_at(1, mine), qkv_at(1, mine), to_x))
    far_qkv_y = started(remote(qkv_at(1, mine), qkv_at(1, mine), to_y))
    ffn_x.wait_recv()
    relay.append(started(remote(ffn_at(mine ^ 1, 0), ffn_at(mine ^ 1, 0), to_y)))
    ffn_y.wait_recv()
    relay.append(started(remote(ffn_at(mine ^ 2, 1), ffn_at(mine ^ 2, 1), to_x)))
    row_z.wait_recv()
    far_rows = row_ref.at[pl.ds(2 * share, share), :]
    row_d = started(remote(far_rows, row_ref.at[pl.ds(3 * share, share), :], to_core))
    out_z.wait_recv()
    far_out_x = started(remote(out_at(1, mine), out_at(1, mine), to_x))
    far_out_y = started(remote(out_at(1, mine), out_at(1, mine), to_y))
    far_qkv_x.wait_recv()
    relay.append(started(remote(qkv_at(1, mine ^ 1, 0), qkv_at(1, mine ^ 1, 0), to_y)))
    far_qkv_y.wait_recv()
    relay.append(started(remote(qkv_at(1, mine ^ 2, 1), qkv_at(1, mine ^ 2, 1), to_x)))
    far_out_x.wait_recv()
    relay.append(started(remote(out_at(1, mine ^ 1, 0), out_at(1, mine ^ 1, 0), to_y)))
    far_out_y.wait_recv()
    relay.append(started(remote(out_at(1, mine ^ 2, 1), out_at(1, mine ^ 2, 1), to_x)))

    for copy in (row_c, row_d, gate_z, *small, *relay):
        copy.wait_recv()
    for copy in (
        qkv_x, qkv_y, out_x, out_y, qkv_z, row_z, row_c, out_z, gate_z, row_d,
        far_qkv_x, far_qkv_y, far_out_x, far_out_y, ffn_x, ffn_y, *small, *relay,
    ):
        copy.wait_send()
    for copy in (keep_qkv, keep_out, keep_ffn, vec_own):
        copy.wait()


def first_exchange(stream, qkv, out, ffn, vectors, bias):
    tokens, quarter = stream.shape
    width = quarter * 4
    hbm = pl.BlockSpec(memory_space=pl.ANY)
    copies = 40
    return pl.pallas_call(
        first_exchange_kernel,
        in_specs=[hbm] * 6,
        out_specs=[hbm] * 7,
        out_shape=[
            jax.ShapeDtypeStruct((tokens, width), bf16),
            jax.ShapeDtypeStruct((2, 3, width, qkv.shape[2]), bf16),
            jax.ShapeDtypeStruct((2, out.shape[0], width), bf16),
            jax.ShapeDtypeStruct((ffn.shape[0], width), bf16),
            jax.ShapeDtypeStruct((ffn.shape[0] // 3 * 2, ffn.shape[1]), bf16),
            jax.ShapeDtypeStruct((4,) + vectors.shape, f32),
            jax.ShapeDtypeStruct(bias.shape, f32),
        ],
        scratch_shapes=[
            pltpu.SemaphoreType.DMA((copies,)),
            pltpu.SemaphoreType.DMA((copies,)),
            pltpu.SemaphoreType.DMA((5,)),
        ],
        compiler_params=pltpu.CompilerParams(collective_id=1, has_side_effects=True),
        name="first_exchange",
    )(stream, qkv, out, ffn, vectors, bias)


def layer_norm(resid):
    centred = resid - jnp.mean(resid, axis=1, keepdims=True)
    inverse = lax.rsqrt(jnp.mean(centred * centred, axis=1, keepdims=True) + norm_eps)
    return centred * inverse, inverse


def norm_backward(grad_in, unit, inverse, gain):
    grad_unit = grad_in * gain
    first = jnp.mean(grad_unit, axis=1, keepdims=True)
    second = jnp.mean(grad_unit * unit, axis=1, keepdims=True)
    grad_resid = inverse * (grad_unit - first - unit * second)
    return grad_resid, jnp.sum(grad_in * unit, axis=0), jnp.sum(grad_in, axis=0)


def gelu_parts(gate):
    root = math.sqrt(2.0 / math.pi)
    inner = jnp.tanh(root * (gate + 0.044715 * gate * gate * gate))
    half = 0.5 * (1.0 + inner)
    slope = half + 0.5 * gate * (1.0 - inner * inner) * root * (1.0 + 3 * 0.044715 * gate * gate)
    return gate * half, slope


def nt(a, b):
    return lax.dot_general(a, b, (((1,), (1,)), ((), ())), preferred_element_type=f32)


def nn(a, b):
    return jnp.dot(a, b, preferred_element_type=f32)


def tn(a, b):
    return lax.dot_general(a, b, (((0,), (0,)), ((), ())), preferred_element_type=f32)


def body(
    square,
    stream,
    chain_ids,
    valid_slots,
    w_qkv,
    b_qkv,
    w_out,
    gain_one,
    bias_one,
    w_up,
    w_down,
    gain_two,
    bias_two,
    cotangent,
):
    c, zh, zl = (lax.axis_index(a) for a in TEAM)
    tokens, quarter = stream.shape
    width = quarter * 4
    share = tokens // 4
    plane = ("y", "x") if square else ("plane",)
    units_here = w_down.shape[0] // 2

    def block_order(parts, key):
        size = parts[0].shape[-1]
        out = jnp.zeros(parts[0].shape[:-1] + (size * 4,), parts[0].dtype)
        for k, part in enumerate(parts):
            start = (0,) * (out.ndim - 1) + ((k ^ key) * size,)
            out = lax.dynamic_update_slice(out, part, start)
        return out

    def send_rows(values, pieces):
        parts = []
        for k1, k2 in CORNERS:
            to_core, to_zl = zh ^ k1, zl ^ k2
            sent = [
                lax.dynamic_slice_in_dim(values, (to_core * 2 + (to_zl ^ h)) * share, share, 0)
                for h in range(pieces)
            ]
            sent = jnp.concatenate(sent, axis=0) if pieces > 1 else sent[0]
            parts.append(lax.ppermute(sent, TEAM, to_team(k1, k2)))
        return block_order(parts, c * 2 + zl)

    head_cols = quarter // 2
    qkv_piece = core_exchange(w_qkv, 2, 1)
    out_piece = core_exchange(w_out, 0, 1)
    up_t = jnp.transpose(w_up, (1, 2, 0))
    kept, given = zip(halves_by_core(up_t[0], 0), halves_by_core(up_t[1], 0), halves_by_core(w_down, 0))
    ffn_piece = by_core(jnp.concatenate(kept, axis=0), swap(jnp.concatenate(given, axis=0), "core"), 1)
    vectors = jnp.stack([gain_one, bias_one, gain_two, bias_two])
    own_bias = lax.dynamic_slice_in_dim(b_qkv, c * head_cols, head_cols, 1)
    third = units_here
    if square:
        stream_row, qkv_full, out_full, ffn_near, gate_far, vectors, far_bias = first_exchange(
            stream,
            qkv_piece,
            out_piece,
            ffn_piece,
            jnp.pad(vectors, ((0, 4), (0, 0))),
            jnp.pad(own_bias, ((0, 5), (0, 0))),
        )
        qkv_bias = (own_bias, far_bias[:3])
        vectors = jnp.transpose(vectors, (1, 0, 2)).reshape(8, width)
        out_full = out_full.reshape(2 * head_cols, width)
        stream_own = stream_row[:share]
        down_far = swap(after(ffn_piece, gate_far)[2 * third :], "zh")
    else:
        both = jnp.concatenate([out_piece, swap(out_piece, "zh")], axis=0)
        out_full = plane_gather(both, 1, plane)
        qkv_full = jnp.stack([plane_gather(qkv_piece, 1, plane), plane_gather(swap(qkv_piece, "zh"), 1, plane)])
        ffn_near = plane_gather(ffn_piece, 1, plane)
        gate_far, down_far = swap(ffn_piece[: 2 * third], "zh"), swap(ffn_piece[2 * third :], "zh")
        qkv_bias = (own_bias, swap(own_bias, "zh"))
        pair = swap(vectors, "zl")
        vectors = block_order([vectors, pair, swap(vectors, "zh"), swap(pair, "zh")], zh * 2 + zl)
        mine = send_rows(stream, 2)
        theirs = swap(mine, "core")
        stream_row = jnp.concatenate([mine[:share], theirs[:share], mine[share:], theirs[share:]], axis=0)
        stream_own = mine[:share]
    gate_far = plane_gather(gate_far, 1, plane)
    gain_one, bias_one, gain_two, bias_two = (vectors[i : i + 1] for i in range(4))

    both_rows = jnp.stack([chain_ids, valid_slots])
    row_ids = jnp.where(c == zh, both_rows, swap(both_rows, "core"))
    chain_row, live_row = row_ids[0], row_ids[1]
    slot = jnp.arange(tokens, dtype=jnp.int32)
    same = chain_row[:, None] == chain_row[None, :]
    earlier = slot[None, :] < slot[:, None]
    positions = jnp.sum(jnp.where(same & earlier, 1, 0), axis=1).astype(jnp.int32)
    table = jnp.stack([chain_row, live_row, positions]).reshape(3, 4, share)

    def chunk(values, axis, j):
        o, h = j % 2, j // 2
        at = (c ^ o) * 2 + (zl ^ h)
        return lax.dynamic_slice_in_dim(values, at, 1, axis)

    table = jnp.concatenate([chunk(table, 1, j) for j in range(4)], axis=1).reshape(3, tokens)
    chain, live_int, positions = table[0], table[1], table[2]
    key_code = jnp.where(live_int > 0, chain, -1)[:, None]
    query_code = jnp.where(live_int > 0, chain, -2)[None, :]
    live = live_int[:share].astype(f32)[:, None]
    half_dim = HEAD_DIM // 2
    frequency = rope_base ** (-2.0 * jnp.arange(half_dim, dtype=f32) / HEAD_DIM)
    angles = positions.astype(f32)[:, None] * frequency[None, :]
    cosine, sine = jnp.cos(angles), jnp.sin(angles)
    cos = jnp.concatenate([cosine, cosine], axis=1)
    sin = jnp.concatenate([-sine, sine], axis=1)

    heads = []
    for r in (0, 1):
        q, k, v = qkv_project(stream_row, qkv_full, r, qkv_bias[r], cos, sin)
        mixed, lse = attend(q, k, v, key_code, query_code)
        heads.append((q, k, v, mixed, lse))
    mixed = after(jnp.concatenate([heads[0][3], heads[1][3]], axis=1), down_far)
    down_far = plane_gather(down_far, 1, plane)
    gate_full = jnp.concatenate([ffn_near[:third], gate_far[:third]], axis=0)
    upper_full = jnp.concatenate([ffn_near[third : 2 * third], gate_far[third:]], axis=0)
    down_full = jnp.concatenate([ffn_near[2 * third :], down_far], axis=0)
    far = chip_sum(nn(mixed[2 * share :], out_full).astype(bf16))
    near = nn(mixed[: 2 * share], out_full).astype(bf16)
    cotangent = after(cotangent, far)
    branch = team_scatter(near, far)
    resid_one = deep_alpha * stream_own.astype(f32) + branch
    unit_one, inverse_one = layer_norm(resid_one)
    normed = unit_one * gain_one + bias_one

    unit = jnp.arange(units_here, dtype=jnp.int32)
    number = [((zh ^ r) * 2 + zl) * (2 * units_here) + c * units_here + unit for r in (0, 1)]
    unit_mask = (jnp.concatenate(number) < FF).astype(f32)[None, :]
    normed_half = team_gather(after(normed.astype(bf16), gate_full, upper_full))
    cot = send_rows(cotangent, 1)
    hidden_half, slope_half, value_half, ffn_half = [], [], [], [None, None]
    for h in (0, 1):
        gate = nt(normed_half[h], gate_full)
        upper = nt(normed_half[h], upper_full)
        value, slope = gelu_parts(gate)
        hidden_half.append((value * upper * unit_mask).astype(bf16))
        slope_half.append((slope * upper * unit_mask).astype(bf16))
        value_half.append((value * unit_mask).astype(bf16))
    for h in (1, 0):
        ffn_half[h] = nn(after(hidden_half[h], cot), down_full).astype(bf16)
    ffn = team_scatter(ffn_half[0], chip_sum(ffn_half[1]))
    resid_two = deep_alpha * normed + ffn
    unit_two, inverse_two = layer_norm(resid_two)
    output = (unit_two * gain_two + bias_two).astype(bf16)

    def return_rows(own):
        out = jnp.zeros((4, share, quarter), own.dtype)
        for k1, k2 in CORNERS:
            block = ((c ^ k1) * 2 + (zl ^ k2))
            sent = lax.dynamic_slice_in_dim(own, block * quarter, quarter, 1)
            got = lax.ppermute(sent, TEAM, from_team(k1, k2))
            out = lax.dynamic_update_slice(out, got[None], ((zh ^ k1) * 2 + (zl ^ k2), 0, 0))
        return out.reshape(tokens, quarter)

    output = return_rows(output)

    grad_output = cot.astype(f32) * live
    grad_resid_two, gain_two_part, bias_two_part = norm_backward(
        grad_output, unit_two, inverse_two, gain_two
    )
    ffn_grad_half = team_gather(grad_resid_two.astype(bf16))
    grad_units_half, back_half = [], [None, None]
    which = lax.broadcasted_iota(jnp.int32, (2, 1, 1), 0)
    for h in (0, 1):
        grad_hidden = nt(ffn_grad_half[h], down_full)
        factor = jnp.where(which == 0, slope_half[h][None], value_half[h][None])
        grad_units_half.append((grad_hidden[None] * factor.astype(f32)).astype(bf16))

    def weight_grad(own, other):
        return core_return(added(own, other).astype(bf16), 0, 1)

    ffn_grad = jnp.concatenate(ffn_grad_half, axis=0)
    hidden = jnp.concatenate(hidden_half, axis=0)
    down_grad = tn(hidden, ffn_grad).astype(bf16)
    down_piece = plane_scatter(down_grad, 1, plane)
    normed_wide = jnp.concatenate(normed_half, axis=0)
    grad_units_half[1] = after(grad_units_half[1], down_grad)
    for h in (1, 0):
        grad_units = grad_units_half[h]
        back_half[h] = (nn(grad_units[0], gate_full) + nn(grad_units[1], upper_full)).astype(bf16)
    back_far = chip_sum(back_half[1])
    up_grad = lax.dot_general(
        jnp.concatenate(grad_units_half, axis=1),
        after(normed_wide, back_half[0], back_far),
        (((1,), (0,)), ((), ())),
        preferred_element_type=f32,
    )
    up_grad = up_grad.astype(bf16).reshape(-1, width)
    grad_normed = deep_alpha * grad_resid_two + team_scatter(back_half[0], back_far)

    grad_normed = after(grad_normed, up_grad, down_piece)
    grad_resid_one, gain_one_part, bias_one_part = norm_backward(
        grad_normed, unit_one, inverse_one, gain_one
    )
    branch_grad_half = team_gather(grad_resid_one.astype(bf16))
    branch_grad = jnp.concatenate(branch_grad_half, axis=0)
    up_piece = plane_scatter(after(up_grad, branch_grad), 1, plane).reshape(2, 2, units_here, -1)
    grad_mixed = nt(branch_grad, out_full).astype(bf16)
    out_grad = tn(mixed, branch_grad).astype(bf16)
    grad_mixed = after(grad_mixed, out_grad, down_piece, output)
    grad_proj, qkv_grad, qkv_sum = [None, None], [None, None], [None, None]
    for r in (1, 0):
        q, k, v, _, lse = heads[r]
        if r == 0:
            down_swapped = swap(down_piece[units_here:], "zh")
            grad_mixed = after(grad_mixed, qkv_grad[1], down_swapped, up_piece)
        grads = attend_back(
            q, k, v, grad_mixed[:, r * head_cols : (r + 1) * head_cols], key_code, query_code, lse, cos, sin
        )
        grad_proj[r] = jnp.concatenate(grads, axis=1)
        qkv_grad[r] = tn(stream_row, grad_proj[r]).astype(bf16)
    gate_swapped = swap(up_piece[0, 1], "zh")
    upper_swapped = swap(up_piece[1, 1], "zh")

    qkv_bias_part = jnp.zeros((3, width), f32)
    for r in (0, 1):
        part = jnp.sum(grad_proj[r].astype(f32), axis=0).reshape(3, head_cols)
        at = ((zh ^ r) * 2 + zl) * quarter + c * head_cols
        qkv_bias_part = lax.dynamic_update_slice(qkv_bias_part, part, (0, at))
    square_sums = jnp.stack(
        [
            jnp.sum(live * resid_one * resid_one),
            jnp.sum(live * branch * branch),
            jnp.sum(live * ffn * ffn),
            jnp.sum(live) * width,
        ]
    )
    norm_parts = jnp.stack([gain_one_part, bias_one_part, gain_two_part, bias_two_part])
    sums = jnp.concatenate([norm_parts, qkv_bias_part, jnp.pad(square_sums[None], ((0, 0), (0, width - 4)))])
    sums = after(sums, upper_swapped)
    for axis in TEAM:
        sums = sums + swap(sums, axis)
    if square:
        for axis in plane:
            sums = sums + swap(sums, axis)
    else:
        sums = lax.psum(sums, plane)
    grad_down = weight_grad(down_piece[:units_here], down_swapped)
    out_sum = plane_scatter(after(out_grad, up_piece, grad_proj[0]), 1, plane)
    for r in (1, 0):
        qkv_sum[r] = plane_scatter(after(qkv_grad[r], up_piece, grad_proj[0]), 0, plane)
    grad_gate_w = weight_grad(up_piece[0, 0], gate_swapped)
    grad_upper_w = weight_grad(up_piece[1, 0], upper_swapped)
    out_swapped = swap(out_sum[head_cols:], "zh")
    grad_out = weight_grad(out_sum[:head_cols], out_swapped)
    qkv_swapped = swap(qkv_sum[1], "zh")
    rows_piece = added(qkv_sum[0], qkv_swapped).astype(bf16)
    rows_piece = rows_piece.reshape(rows_piece.shape[0], 3, head_cols)
    grad_qkv = jnp.transpose(core_return(rows_piece, 2, 0), (1, 0, 2)).astype(f32)

    weight_r = [jnp.concatenate([qkv_full[r][i] for i in range(3)], axis=1) for r in (0, 1)]

    def stream_part(h):
        rows = slice(h * 2 * share, (h + 1) * 2 * share)
        return (nt(grad_proj[0][rows], weight_r[0]) + nt(grad_proj[1][rows], weight_r[1])).astype(bf16)

    grad_proj[1] = after(grad_proj[1], gate_swapped)
    far = after(chip_sum(stream_part(1)), upper_swapped)
    near = stream_part(0)
    grad_stream = (deep_alpha * grad_resid_one + team_scatter(near, far)).astype(bf16)
    grad_stream = return_rows(after(grad_stream, out_swapped))

    mine = lax.dynamic_slice_in_dim(sums[:7], (zh * 2 + zl) * quarter, quarter, 1)
    stream_stats = jnp.sqrt(sums[7, :3] / sums[7, 3])

    grad_up = jnp.stack([grad_gate_w, grad_upper_w]).astype(bf16)
    grad_up = jnp.transpose(grad_up, (2, 0, 1)).astype(f32)
    return (
        output,
        grad_stream,
        grad_qkv,
        mine[4:7],
        grad_out.astype(f32),
        mine[0],
        mine[1],
        grad_up,
        grad_down.astype(f32),
        mine[2],
        mine[3],
        stream_stats,
    )


def solution(mesh):
    wide, narrow = mesh.shape["wide"], mesh.shape["narrow"]
    square = wide == 8
    if square:
        plane, dims = ("y", "x"), (2, 2)
    else:
        plane, dims = ("plane",), (wide // 2,)
    fine = Mesh(mesh.devices.reshape(dims + (2, 2, narrow // 2)), plane + TEAM)
    w, n = plane + ("core",), ("zh", "zl")
    placed = (
        P(w, n),
        P(w),
        P(w),
        P(None, w, n),
        P(None, n),
        P(n, w),
        P(n),
        P(n),
        P(w, None, n),
        P(n, w),
        P(n),
        P(n),
        P(w, n),
    )
    return jax.shard_map(
        functools.partial(body, square),
        mesh=fine,
        in_specs=placed,
        out_specs=(
            P(w, n),
            P(w, n),
            P(None, w, n),
            P(None, n),
            P(n, w),
            P(n),
            P(n),
            P(w, None, n),
            P(n, w),
            P(n),
            P(n),
            P(),
        ),
        check_vma=False,
    )
```

```python
import functools
import math

import jax
import jax.numpy as jnp
import numpy as np
from jax import lax
from jax.experimental import pallas as pl
from jax.experimental.pallas import tpu as pltpu
from jax.sharding import Mesh
from jax.sharding import PartitionSpec as P

HEAD_DIM = 128
FF = 5461

deep_alpha = 6.928203230275509
norm_eps = 1e-05
mask_value = -1e30
rope_base = 10000.0
score_scale = 1.0 / math.sqrt(HEAD_DIM)

f32 = jnp.float32
bf16 = jnp.bfloat16
SWAP = [(0, 1), (1, 0)]


def swap(values, axis):
    return lax.ppermute(values, axis, SWAP)


def qkv_kernel(s_ref, w_ref, b_ref, cos_ref, sin_ref, q_ref, k_ref, v_ref):
    rows = s_ref[...]
    cos, sin = cos_ref[...], sin_ref[...]
    for c, out in enumerate((q_ref, k_ref, v_ref)):
        acc = jnp.dot(rows, w_ref[0, c], preferred_element_type=f32) + b_ref[c : c + 1, :]
        if c == 2:
            out[...] = acc.astype(bf16)
            continue
        for h in range(acc.shape[1] // HEAD_DIM):
            cols = slice(h * HEAD_DIM, (h + 1) * HEAD_DIM)
            head = acc[:, cols]
            turned = pltpu.roll(head, HEAD_DIM // 2, 1)
            out[:, cols] = (head * cos + turned * sin).astype(bf16)


def qkv_project(stream_row, weight, r, bias, cos, sin):
    tokens, depth = stream_row.shape
    cols = weight.shape[3]
    tile = 256
    shape = jax.ShapeDtypeStruct((tokens, cols), bf16)
    return pl.pallas_call(
        qkv_kernel,
        grid=(tokens // tile,),
        in_specs=[
            pl.BlockSpec((tile, depth), lambda i: (i, 0)),
            pl.BlockSpec((1, 3, depth, cols), lambda i: (r, 0, 0, 0)),
            pl.BlockSpec((3, cols), lambda i: (0, 0)),
            pl.BlockSpec((tile, HEAD_DIM), lambda i: (i, 0)),
            pl.BlockSpec((tile, HEAD_DIM), lambda i: (i, 0)),
        ],
        out_specs=[pl.BlockSpec((tile, cols), lambda i: (i, 0))] * 3,
        out_shape=[shape] * 3,
        name="qkv_project",
        cost_estimate=pl.CostEstimate(
            flops=2 * tokens * depth * 3 * cols,
            bytes_accessed=2 * (tokens * depth + 3 * depth * cols + 3 * tokens * cols),
            transcendentals=0,
        ),
    )(stream_row, weight, bias, cos, sin)


def allowed_of(key_code, query_code):
    return (key_code == query_code) | ((query_code < 0) & (key_code >= 0))


def attend_kernel(q_ref, k_ref, v_ref, kc_ref, qc_ref, o_ref, lse_ref):
    scores = lax.dot_general(
        k_ref[...], q_ref[...], (((1,), (1,)), ((), ())), preferred_element_type=f32
    )
    scores = jnp.where(allowed_of(kc_ref[...], qc_ref[...]), scores * score_scale, mask_value)
    top = jnp.max(scores, axis=0, keepdims=True)
    weights = jnp.exp(scores - top)
    total = jnp.sum(weights, axis=0, keepdims=True)
    mixed = lax.dot_general(
        v_ref[...], weights.astype(bf16), (((0,), (0,)), ((), ())), preferred_element_type=f32
    )
    o_ref[...] = jnp.transpose(mixed / total).astype(bf16)
    lse_ref[0] = top + jnp.log(total)


def attend(query, keys, value, key_code, query_code):
    tokens, cols = query.shape
    heads = cols // HEAD_DIM
    tile = 256
    per_q = pl.BlockSpec((tile, HEAD_DIM), lambda h, i: (i, h))
    per_head = pl.BlockSpec((tokens, HEAD_DIM), lambda h, i: (0, h))
    return pl.pallas_call(
        attend_kernel,
        grid=(heads, tokens // tile),
        in_specs=[
            per_q,
            per_head,
            per_head,
            pl.BlockSpec((tokens, 1), lambda h, i: (0, 0)),
            pl.BlockSpec((1, tile), lambda h, i: (0, i)),
        ],
        out_specs=[per_q, pl.BlockSpec((1, 1, tile), lambda h, i: (h, 0, i))],
        out_shape=[
            jax.ShapeDtypeStruct((tokens, cols), bf16),
            jax.ShapeDtypeStruct((heads, 1, tokens), f32),
        ],
        name="attend",
        cost_estimate=pl.CostEstimate(
            flops=4 * tokens * tokens * cols,
            bytes_accessed=8 * tokens * cols,
            transcendentals=heads * tokens * tokens,
        ),
    )(query, keys, value, key_code, query_code)


def attend_back_kernel(
    q_ref, k_ref, v_ref, g_ref, kc_ref, qc_ref, lse_ref, cosq_ref, sinq_ref, cosk_ref, sink_ref,
    dq_ref, dk_ref, dv_ref, dk_acc, dv_acc,
):
    step = pl.program_id(1)

    @pl.when(step == 0)
    def _():
        dk_acc[...] = jnp.zeros_like(dk_acc)
        dv_acc[...] = jnp.zeros_like(dv_acc)

    query, keys, grads = q_ref[...], k_ref[...], g_ref[...]
    nt = (((1,), (1,)), ((), ()))
    scores = lax.dot_general(keys, query, nt, preferred_element_type=f32)
    scores = jnp.where(allowed_of(kc_ref[...], qc_ref[...]), scores * score_scale, mask_value)
    probs = jnp.exp(scores - lse_ref[0])
    grad_probs = lax.dot_general(v_ref[...], grads, nt, preferred_element_type=f32)
    mean = jnp.sum(probs * grad_probs, axis=0, keepdims=True)
    grad_scores = (probs * (grad_probs - mean)).astype(bf16)
    dv_acc[...] += jnp.dot(probs.astype(bf16), grads, preferred_element_type=f32)
    dk_acc[...] += jnp.dot(grad_scores, query, preferred_element_type=f32)
    dq = jnp.transpose(
        lax.dot_general(keys, grad_scores, (((0,), (0,)), ((), ())), preferred_element_type=f32)
    )
    dq = dq * score_scale
    half = HEAD_DIM // 2
    dq_ref[...] = (dq * cosq_ref[...] - pltpu.roll(dq, half, 1) * sinq_ref[...]).astype(bf16)

    @pl.when(step == pl.num_programs(1) - 1)
    def _():
        dk = dk_acc[...] * score_scale
        dk_ref[...] = (dk * cosk_ref[...] - pltpu.roll(dk, half, 1) * sink_ref[...]).astype(bf16)
        dv_ref[...] = dv_acc[...].astype(bf16)


def attend_back(query, keys, value, grad_mixed, key_code, query_code, lse, cos, sin):
    tokens, cols = query.shape
    heads = cols // HEAD_DIM
    tile = 256
    per_q = pl.BlockSpec((tile, HEAD_DIM), lambda h, i: (i, h))
    per_head = pl.BlockSpec((tokens, HEAD_DIM), lambda h, i: (0, h))
    table_q = pl.BlockSpec((tile, HEAD_DIM), lambda h, i: (i, 0))
    table = pl.BlockSpec((tokens, HEAD_DIM), lambda h, i: (0, 0))
    return pl.pallas_call(
        attend_back_kernel,
        grid=(heads, tokens // tile),
        in_specs=[
            per_q,
            per_head,
            per_head,
            per_q,
            pl.BlockSpec((tokens, 1), lambda h, i: (0, 0)),
            pl.BlockSpec((1, tile), lambda h, i: (0, i)),
            pl.BlockSpec((1, 1, tile), lambda h, i: (h, 0, i)),
            table_q,
            table_q,
            table,
            table,
        ],
        out_specs=[per_q, per_head, per_head],
        out_shape=[jax.ShapeDtypeStruct((tokens, cols), bf16)] * 3,
        scratch_shapes=[pltpu.VMEM((tokens, HEAD_DIM), f32)] * 2,
        name="attend_back",
        cost_estimate=pl.CostEstimate(
            flops=10 * tokens * tokens * cols,
            bytes_accessed=14 * tokens * cols,
            transcendentals=heads * tokens * tokens,
        ),
    )(query, keys, value, grad_mixed, key_code, query_code, lse, cos, sin, cos, sin)


def by_core(mine, other, axis):
    c, size = lax.axis_index("core"), mine.shape[axis]
    shape = list(mine.shape)
    shape[axis] = 2 * size
    out = lax.dynamic_update_slice_in_dim(jnp.zeros(shape, mine.dtype), mine, c * size, axis)
    return lax.dynamic_update_slice_in_dim(out, other, (1 - c) * size, axis)


def halves_by_core(values, axis):
    size = values.shape[axis] // 2
    c = lax.axis_index("core")
    return (
        lax.dynamic_slice_in_dim(values, c * size, size, axis),
        lax.dynamic_slice_in_dim(values, (1 - c) * size, size, axis),
    )


def core_exchange(shard, axis_units, axis_rows):
    keep, give = halves_by_core(shard, axis_units)
    return by_core(keep, swap(give, "core"), axis_rows)


def core_return(piece, axis_units, axis_rows):
    keep, give = halves_by_core(piece, axis_rows)
    return by_core(keep, swap(give, "core"), axis_units)


def plane_gather(piece, axis, plane):
    return lax.all_gather(piece, plane, axis=axis, tiled=True)


def plane_scatter(product, axis, plane):
    return lax.psum_scatter(product, plane, scatter_dimension=axis, tiled=True)


def added(*terms):
    total = terms[0].astype(f32)
    for term in terms[1:]:
        total = total + term.astype(f32)
    return total


def after(values, *earlier):
    return lax.optimization_barrier((values, *earlier))[0]


def team_gather(own):
    core = swap(own, "core")
    chip = swap(own, "zl")
    return (
        jnp.concatenate([own, core], axis=0),
        jnp.concatenate([chip, swap(chip, "core")], axis=0),
    )


def chip_sum(far):
    share = far.shape[0] // 2
    return added(far[:share], swap(far[share:].astype(bf16), "core")).astype(bf16)


def team_scatter(near, far_sum):
    share = far_sum.shape[0]
    from_chip = swap(far_sum, "zl")
    from_core = swap(near[share:].astype(bf16), "core")
    return added(near[:share], from_core, from_chip)


TEAM = ("core", "zh", "zl")


def team_index(c, zh, zl):
    return c * 4 + zh * 2 + zl


def to_team(k1, k2):
    return [
        (team_index(c, h, q), team_index(h ^ k1, c, q ^ k2))
        for c in (0, 1)
        for h in (0, 1)
        for q in (0, 1)
    ]


def from_team(k1, k2):
    return [(b, a) for a, b in to_team(k1, k2)]


CORNERS = [(0, 0), (0, 1), (1, 0), (1, 1)]


def first_exchange_kernel(
    stream_ref, qkv_ref, out_ref, ffn_ref, vec_ref, bias_ref,
    row_ref, qkv_full_ref, out_full_ref, ffn_full_ref, gate_ref, vecs_ref, bias_far_ref,
    send, recv, local,
):
    y, x = lax.axis_index("y"), lax.axis_index("x")
    c, zh, zl = (lax.axis_index(a) for a in TEAM)
    z = zh * 2 + zl
    mine = y * 2 + x
    share = row_ref.shape[0] // 4
    quarter = stream_ref.shape[1]
    rows = qkv_ref.shape[1]
    units = out_ref.shape[0]
    to_x, to_y = {"x": 1 - x}, {"y": 1 - y}
    to_core, to_zl, to_zh = {"core": 1 - c}, {"zl": 1 - zl}, {"zh": 1 - zh}
    both_z = {"zh": 1 - zh, "zl": 1 - zl}

    barrier = pltpu.get_barrier_semaphore()

    def greet(device):
        pl.semaphore_signal(barrier, inc=1, device_id=device, device_id_type=pl.DeviceIdType.MESH)

    greet(to_x)
    greet(to_y)
    for flip in range(1, 8):
        greet({"core": c ^ (flip >> 2), "zh": zh ^ ((flip >> 1) & 1), "zl": zl ^ (flip & 1)})
    pl.semaphore_wait(barrier, 9)

    used = [0]

    def remote(src, dst, device):
        i = used[0]
        used[0] += 1
        return pltpu.make_async_remote_copy(
            src_ref=src,
            dst_ref=dst,
            send_sem=send.at[i],
            recv_sem=recv.at[i],
            device_id=device,
            device_id_type=pl.DeviceIdType.MESH,
        )

    def started(copy):
        copy.start()
        return copy

    def block(i):
        return pl.ds(pl.multiple_of(i * quarter, quarter), quarter)

    def qkv_at(r, owner, half=None):
        if half is None:
            return qkv_full_ref.at[r, :, pl.ds(pl.multiple_of(owner * rows, rows), rows), :]
        size = rows // 2
        return qkv_full_ref.at[
            r, :, pl.ds(pl.multiple_of(owner * rows + half * size, size), size), :
        ]

    def out_at(r, owner, half=None):
        if half is None:
            return out_full_ref.at[r, :, block(owner)]
        size = units // 2
        return out_full_ref.at[r, pl.ds(half * size, size), block(owner)]

    def ffn_at(owner, half=None):
        if half is None:
            return ffn_full_ref.at[:, block(owner)]
        size = ffn_ref.shape[0] // 2
        return ffn_full_ref.at[pl.ds(half * size, size), block(owner)]

    def chunk_copies(values_ref, target_ref):
        copies = []
        for k1, k2 in CORNERS:
            core_to, zl_to = zh ^ k1, zl ^ k2
            at = pl.multiple_of((core_to * 2 + zl_to) * share, share)
            copies.append(
                remote(
                    values_ref.at[pl.ds(at, share), :],
                    target_ref.at[pl.ds(0, share), block(z)],
                    {"core": core_to, "zh": c, "zl": zl_to},
                )
            )
        at = pl.multiple_of((c * 2 + zl) * share, share)
        stays = pltpu.make_async_copy(
            values_ref.at[pl.ds(at, share), :],
            target_ref.at[pl.ds(0, share), block(z)],
            local.at[2],
        )
        return copies, stays

    def start_chunks(copies, stays):
        @pl.when(c == zh)
        def _():
            stays.start()

        @pl.when(c != zh)
        def _():
            copies[0].start()

        for copy in copies[1:]:
            copy.start()

    def wait_chunks(copies, stays):
        @pl.when(c == zh)
        def _():
            stays.wait()

        @pl.when(c != zh)
        def _():
            copies[0].wait()

        for copy in copies[1:]:
            copy.wait()

    stream_copies, stream_stays = chunk_copies(stream_ref, row_ref)
    start_chunks(stream_copies, stream_stays)
    qkv_x = started(remote(qkv_ref, qkv_at(0, mine), to_x))
    qkv_y = started(remote(qkv_ref, qkv_at(0, mine), to_y))
    out_x = started(remote(out_ref, out_at(0, mine), to_x))
    out_y = started(remote(out_ref, out_at(0, mine), to_y))
    keep_qkv = pltpu.make_async_copy(qkv_ref, qkv_at(0, mine), local.at[0])
    keep_out = pltpu.make_async_copy(out_ref, out_at(0, mine), local.at[1])
    keep_ffn = pltpu.make_async_copy(ffn_ref, ffn_at(mine), local.at[4])
    keep_qkv.start()
    keep_out.start()
    keep_ffn.start()
    ffn_x = started(remote(ffn_ref, ffn_at(mine), to_x))
    ffn_y = started(remote(ffn_ref, ffn_at(mine), to_y))
    qkv_z = started(remote(qkv_ref, qkv_at(1, mine), to_zh))
    small = []
    for device in (to_zl, to_zh, both_z):
        small.append(started(remote(vec_ref, vecs_ref.at[z], device)))
    small.append(started(remote(bias_ref, bias_far_ref, to_zh)))
    vec_own = pltpu.make_async_copy(vec_ref, vecs_ref.at[z], local.at[3])
    vec_own.start()

    qkv_x.wait_recv()
    relay = [started(remote(qkv_at(0, mine ^ 1, 0), qkv_at(0, mine ^ 1, 0), to_y))]
    qkv_y.wait_recv()
    relay.append(started(remote(qkv_at(0, mine ^ 2, 1), qkv_at(0, mine ^ 2, 1), to_x)))
    wait_chunks(stream_copies, stream_stays)
    own_rows = row_ref.at[pl.ds(0, share), :]
    row_z = started(remote(own_rows, row_ref.at[pl.ds(2 * share, share), :], to_zl))
    row_c = started(remote(own_rows, row_ref.at[pl.ds(share, share), :], to_core))
    out_z = started(remote(out_ref, out_at(1, mine), to_zh))
    gate_z = started(remote(ffn_ref.at[pl.ds(0, gate_ref.shape[0]), :], gate_ref, to_zh))
    out_x.wait_recv()
    relay.append(started(remote(out_at(0, mine ^ 1, 0), out_at(0, mine ^ 1, 0), to_y)))
    out_y.wait_recv()
    relay.append(started(remote(out_at(0, mine ^ 2, 1), out_at(0, mine ^ 2, 1), to_x)))
    qkv_z.wait_recv()
    far_qkv_x = started(remote(qkv_at(1, mine), qkv_at(1, mine), to_x))
    far_qkv_y = started(remote(qkv_at(1, mine), qkv_at(1, mine), to_y))
    ffn_x.wait_recv()
    relay.append(started(remote(ffn_at(mine ^ 1, 0), ffn_at(mine ^ 1, 0), to_y)))
    ffn_y.wait_recv()
    relay.append(started(remote(ffn_at(mine ^ 2, 1), ffn_at(mine ^ 2, 1), to_x)))
    row_z.wait_recv()
    far_rows = row_ref.at[pl.ds(2 * share, share), :]
    row_d = started(remote(far_rows, row_ref.at[pl.ds(3 * share, share), :], to_core))
    out_z.wait_recv()
    far_out_x = started(remote(out_at(1, mine), out_at(1, mine), to_x))
    far_out_y = started(remote(out_at(1, mine), out_at(1, mine), to_y))
    far_qkv_x.wait_recv()
    relay.append(started(remote(qkv_at(1, mine ^ 1, 0), qkv_at(1, mine ^ 1, 0), to_y)))
    far_qkv_y.wait_recv()
    relay.append(started(remote(qkv_at(1, mine ^ 2, 1), qkv_at(1, mine ^ 2, 1), to_x)))
    far_out_x.wait_recv()
    relay.append(started(remote(out_at(1, mine ^ 1, 0), out_at(1, mine ^ 1, 0), to_y)))
    far_out_y.wait_recv()
    relay.append(started(remote(out_at(1, mine ^ 2, 1), out_at(1, mine ^ 2, 1), to_x)))

    for copy in (row_c, row_d, gate_z, *small, *relay):
        copy.wait_recv()
    for copy in (
        qkv_x, qkv_y, out_x, out_y, qkv_z, row_z, row_c, out_z, gate_z, row_d,
        far_qkv_x, far_qkv_y, far_out_x, far_out_y, ffn_x, ffn_y, *small, *relay,
    ):
        copy.wait_send()
    for copy in (keep_qkv, keep_out, keep_ffn, vec_own):
        copy.wait()


def first_exchange(stream, qkv, out, ffn, vectors, bias):
    tokens, quarter = stream.shape
    width = quarter * 4
    hbm = pl.BlockSpec(memory_space=pl.ANY)
    copies = 40
    return pl.pallas_call(
        first_exchange_kernel,
        in_specs=[hbm] * 6,
        out_specs=[hbm] * 7,
        out_shape=[
            jax.ShapeDtypeStruct((tokens, width), bf16),
            jax.ShapeDtypeStruct((2, 3, width, qkv.shape[2]), bf16),
            jax.ShapeDtypeStruct((2, out.shape[0], width), bf16),
            jax.ShapeDtypeStruct((ffn.shape[0], width), bf16),
            jax.ShapeDtypeStruct((ffn.shape[0] // 3 * 2, ffn.shape[1]), bf16),
            jax.ShapeDtypeStruct((4,) + vectors.shape, f32),
            jax.ShapeDtypeStruct(bias.shape, f32),
        ],
        scratch_shapes=[
            pltpu.SemaphoreType.DMA((copies,)),
            pltpu.SemaphoreType.DMA((copies,)),
            pltpu.SemaphoreType.DMA((5,)),
        ],
        compiler_params=pltpu.CompilerParams(collective_id=1, has_side_effects=True),
        name="first_exchange",
    )(stream, qkv, out, ffn, vectors, bias)


def layer_norm(resid):
    centred = resid - jnp.mean(resid, axis=1, keepdims=True)
    inverse = lax.rsqrt(jnp.mean(centred * centred, axis=1, keepdims=True) + norm_eps)
    return centred * inverse, inverse


def norm_backward(grad_in, unit, inverse, gain):
    grad_unit = grad_in * gain
    first = jnp.mean(grad_unit, axis=1, keepdims=True)
    second = jnp.mean(grad_unit * unit, axis=1, keepdims=True)
    grad_resid = inverse * (grad_unit - first - unit * second)
    return grad_resid, jnp.sum(grad_in * unit, axis=0), jnp.sum(grad_in, axis=0)


def gelu_parts(gate):
    root = math.sqrt(2.0 / math.pi)
    inner = jnp.tanh(root * (gate + 0.044715 * gate * gate * gate))
    half = 0.5 * (1.0 + inner)
    slope = half + 0.5 * gate * (1.0 - inner * inner) * root * (1.0 + 3 * 0.044715 * gate * gate)
    return gate * half, slope


def nt(a, b):
    return lax.dot_general(a, b, (((1,), (1,)), ((), ())), preferred_element_type=f32)


def nn(a, b):
    return jnp.dot(a, b, preferred_element_type=f32)


def tn(a, b):
    return lax.dot_general(a, b, (((0,), (0,)), ((), ())), preferred_element_type=f32)


def body(
    square,
    stream,
    chain_ids,
    valid_slots,
    w_qkv,
    b_qkv,
    w_out,
    gain_one,
    bias_one,
    w_up,
    w_down,
    gain_two,
    bias_two,
    cotangent,
):
    c, zh, zl = (lax.axis_index(a) for a in TEAM)
    tokens, quarter = stream.shape
    width = quarter * 4
    share = tokens // 4
    plane = ("y", "x") if square else ("plane",)
    units_here = w_down.shape[0] // 2

    def block_order(parts, key):
        size = parts[0].shape[-1]
        out = jnp.zeros(parts[0].shape[:-1] + (size * 4,), parts[0].dtype)
        for k, part in enumerate(parts):
            start = (0,) * (out.ndim - 1) + ((k ^ key) * size,)
            out = lax.dynamic_update_slice(out, part, start)
        return out

    def send_rows(values, pieces):
        parts = []
        for k1, k2 in CORNERS:
            to_core, to_zl = zh ^ k1, zl ^ k2
            sent = [
                lax.dynamic_slice_in_dim(values, (to_core * 2 + (to_zl ^ h)) * share, share, 0)
                for h in range(pieces)
            ]
            sent = jnp.concatenate(sent, axis=0) if pieces > 1 else sent[0]
            parts.append(lax.ppermute(sent, TEAM, to_team(k1, k2)))
        return block_order(parts, c * 2 + zl)

    head_cols = quarter // 2
    qkv_piece = core_exchange(w_qkv, 2, 1)
    out_piece = core_exchange(w_out, 0, 1)
    up_t = jnp.transpose(w_up, (1, 2, 0))
    kept, given = zip(halves_by_core(up_t[0], 0), halves_by_core(up_t[1], 0), halves_by_core(w_down, 0))
    ffn_piece = by_core(jnp.concatenate(kept, axis=0), swap(jnp.concatenate(given, axis=0), "core"), 1)
    vectors = jnp.stack([gain_one, bias_one, gain_two, bias_two])
    own_bias = lax.dynamic_slice_in_dim(b_qkv, c * head_cols, head_cols, 1)
    third = units_here
    if square:
        stream_row, qkv_full, out_full, ffn_near, gate_far, vectors, far_bias = first_exchange(
            stream,
            qkv_piece,
            out_piece,
            ffn_piece,
            jnp.pad(vectors, ((0, 4), (0, 0))),
            jnp.pad(own_bias, ((0, 5), (0, 0))),
        )
        qkv_bias = (own_bias, far_bias[:3])
        vectors = jnp.transpose(vectors, (1, 0, 2)).reshape(8, width)
        out_full = out_full.reshape(2 * head_cols, width)
        stream_own = stream_row[:share]
        down_far = swap(after(ffn_piece, gate_far)[2 * third :], "zh")
    else:
        both = jnp.concatenate([out_piece, swap(out_piece, "zh")], axis=0)
        out_full = plane_gather(both, 1, plane)
        qkv_full = jnp.stack([plane_gather(qkv_piece, 1, plane), plane_gather(swap(qkv_piece, "zh"), 1, plane)])
        ffn_near = plane_gather(ffn_piece, 1, plane)
        gate_far, down_far = swap(ffn_piece[: 2 * third], "zh"), swap(ffn_piece[2 * third :], "zh")
        qkv_bias = (own_bias, swap(own_bias, "zh"))
        pair = swap(vectors, "zl")
        vectors = block_order([vectors, pair, swap(vectors, "zh"), swap(pair, "zh")], zh * 2 + zl)
        mine = send_rows(stream, 2)
        theirs = swap(mine, "core")
        stream_row = jnp.concatenate([mine[:share], theirs[:share], mine[share:], theirs[share:]], axis=0)
        stream_own = mine[:share]
    gate_far = plane_gather(gate_far, 1, plane)
    gain_one, bias_one, gain_two, bias_two = (vectors[i : i + 1] for i in range(4))

    both_rows = jnp.stack([chain_ids, valid_slots])
    row_ids = jnp.where(c == zh, both_rows, swap(both_rows, "core"))
    chain_row, live_row = row_ids[0], row_ids[1]
    slot = jnp.arange(tokens, dtype=jnp.int32)
    same = chain_row[:, None] == chain_row[None, :]
    earlier = slot[None, :] < slot[:, None]
    positions = jnp.sum(jnp.where(same & earlier, 1, 0), axis=1).astype(jnp.int32)
    table = jnp.stack([chain_row, live_row, positions]).reshape(3, 4, share)

    def chunk(values, axis, j):
        o, h = j % 2, j // 2
        at = (c ^ o) * 2 + (zl ^ h)
        return lax.dynamic_slice_in_dim(values, at, 1, axis)

    table = jnp.concatenate([chunk(table, 1, j) for j in range(4)], axis=1).reshape(3, tokens)
    chain, live_int, positions = table[0], table[1], table[2]
    key_code = jnp.where(live_int > 0, chain, -1)[:, None]
    query_code = jnp.where(live_int > 0, chain, -2)[None, :]
    live = live_int[:share].astype(f32)[:, None]
    half_dim = HEAD_DIM // 2
    frequency = rope_base ** (-2.0 * jnp.arange(half_dim, dtype=f32) / HEAD_DIM)
    angles = positions.astype(f32)[:, None] * frequency[None, :]
    cosine, sine = jnp.cos(angles), jnp.sin(angles)
    cos = jnp.concatenate([cosine, cosine], axis=1)
    sin = jnp.concatenate([-sine, sine], axis=1)

    heads = []
    for r in (0, 1):
        q, k, v = qkv_project(stream_row, qkv_full, r, qkv_bias[r], cos, sin)
        mixed, lse = attend(q, k, v, key_code, query_code)
        heads.append((q, k, v, mixed, lse))
    mixed = after(jnp.concatenate([heads[0][3], heads[1][3]], axis=1), down_far)
    down_far = plane_gather(down_far, 1, plane)
    gate_full = jnp.concatenate([ffn_near[:third], gate_far[:third]], axis=0)
    upper_full = jnp.concatenate([ffn_near[third : 2 * third], gate_far[third:]], axis=0)
    down_full = jnp.concatenate([ffn_near[2 * third :], down_far], axis=0)
    far = chip_sum(nn(mixed[2 * share :], out_full).astype(bf16))
    near = nn(mixed[: 2 * share], out_full).astype(bf16)
    cotangent = after(cotangent, far)
    branch = team_scatter(near, far)
    resid_one = deep_alpha * stream_own.astype(f32) + branch
    unit_one, inverse_one = layer_norm(resid_one)
    normed = unit_one * gain_one + bias_one

    unit = jnp.arange(units_here, dtype=jnp.int32)
    number = [((zh ^ r) * 2 + zl) * (2 * units_here) + c * units_here + unit for r in (0, 1)]
    unit_mask = (jnp.concatenate(number) < FF).astype(f32)[None, :]
    normed_half = team_gather(after(normed.astype(bf16), gate_full, upper_full))
    cot = send_rows(cotangent, 1)
    hidden_half, slope_half, value_half, ffn_half = [], [], [], [None, None]
    for h in (0, 1):
        gate = nt(normed_half[h], gate_full)
        upper = nt(normed_half[h], upper_full)
        value, slope = gelu_parts(gate)
        hidden_half.append((value * upper * unit_mask).astype(bf16))
        slope_half.append((slope * upper * unit_mask).astype(bf16))
        value_half.append((value * unit_mask).astype(bf16))
    for h in (1, 0):
        ffn_half[h] = nn(after(hidden_half[h], cot), down_full).astype(bf16)
    ffn = team_scatter(ffn_half[0], chip_sum(ffn_half[1]))
    resid_two = deep_alpha * normed + ffn
    unit_two, inverse_two = layer_norm(resid_two)
    output = (unit_two * gain_two + bias_two).astype(bf16)

    def return_rows(own):
        out = jnp.zeros((4, share, quarter), own.dtype)
        for k1, k2 in CORNERS:
            block = ((c ^ k1) * 2 + (zl ^ k2))
            sent = lax.dynamic_slice_in_dim(own, block * quarter, quarter, 1)
            got = lax.ppermute(sent, TEAM, from_team(k1, k2))
            out = lax.dynamic_update_slice(out, got[None], ((zh ^ k1) * 2 + (zl ^ k2), 0, 0))
        return out.reshape(tokens, quarter)

    output = return_rows(output)

    grad_output = cot.astype(f32) * live
    grad_resid_two, gain_two_part, bias_two_part = norm_backward(
        grad_output, unit_two, inverse_two, gain_two
    )
    ffn_grad_half = team_gather(grad_resid_two.astype(bf16))
    grad_units_half, back_half = [], [None, None]
    which = lax.broadcasted_iota(jnp.int32, (2, 1, 1), 0)
    for h in (0, 1):
        grad_hidden = nt(ffn_grad_half[h], down_full)
        factor = jnp.where(which == 0, slope_half[h][None], value_half[h][None])
        grad_units_half.append((grad_hidden[None] * factor.astype(f32)).astype(bf16))

    def weight_grad(own, other):
        return core_return(added(own, other).astype(bf16), 0, 1)

    ffn_grad = jnp.concatenate(ffn_grad_half, axis=0)
    hidden = jnp.concatenate(hidden_half, axis=0)
    down_grad = tn(hidden, ffn_grad).astype(bf16)
    down_piece = plane_scatter(down_grad, 1, plane)
    normed_wide = jnp.concatenate(normed_half, axis=0)
    grad_units_half[1] = after(grad_units_half[1], down_grad)
    for h in (1, 0):
        grad_units = grad_units_half[h]
        back_half[h] = (nn(grad_units[0], gate_full) + nn(grad_units[1], upper_full)).astype(bf16)
    back_far = chip_sum(back_half[1])
    up_grad = lax.dot_general(
        jnp.concatenate(grad_units_half, axis=1),
        after(normed_wide, back_half[0], back_far),
        (((1,), (0,)), ((), ())),
        preferred_element_type=f32,
    )
    up_grad = up_grad.astype(bf16).reshape(-1, width)
    grad_normed = deep_alpha * grad_resid_two + team_scatter(back_half[0], back_far)

    grad_normed = after(grad_normed, up_grad, down_piece)
    grad_resid_one, gain_one_part, bias_one_part = norm_backward(
        grad_normed, unit_one, inverse_one, gain_one
    )
    branch_grad_half = team_gather(grad_resid_one.astype(bf16))
    branch_grad = jnp.concatenate(branch_grad_half, axis=0)
    up_piece = plane_scatter(after(up_grad, branch_grad), 1, plane).reshape(2, 2, units_here, -1)
    grad_mixed = nt(branch_grad, out_full).astype(bf16)
    out_grad = tn(mixed, branch_grad).astype(bf16)
    grad_mixed = after(grad_mixed, out_grad, down_piece, output)
    grad_proj, qkv_grad, qkv_sum = [None, None], [None, None], [None, None]
    for r in (1, 0):
        q, k, v, _, lse = heads[r]
        if r == 0:
            down_swapped = swap(down_piece[units_here:], "zh")
            grad_mixed = after(grad_mixed, qkv_grad[1], down_swapped, up_piece)
        grads = attend_back(
            q, k, v, grad_mixed[:, r * head_cols : (r + 1) * head_cols], key_code, query_code, lse, cos, sin
        )
        grad_proj[r] = jnp.concatenate(grads, axis=1)
        qkv_grad[r] = tn(stream_row, grad_proj[r]).astype(bf16)
    gate_swapped = swap(up_piece[0, 1], "zh")
    upper_swapped = swap(up_piece[1, 1], "zh")

    grad_down = weight_grad(down_piece[:units_here], down_swapped)
    out_sum = plane_scatter(after(out_grad, up_piece, grad_proj[0]), 1, plane)
    for r in (1, 0):
        qkv_sum[r] = plane_scatter(after(qkv_grad[r], up_piece, grad_proj[0]), 0, plane)
    grad_gate_w = weight_grad(up_piece[0, 0], gate_swapped)
    grad_upper_w = weight_grad(up_piece[1, 0], upper_swapped)
    out_swapped = swap(out_sum[head_cols:], "zh")
    grad_out = weight_grad(out_sum[:head_cols], out_swapped)
    qkv_swapped = swap(qkv_sum[1], "zh")
    rows_piece = added(qkv_sum[0], qkv_swapped).astype(bf16)
    rows_piece = rows_piece.reshape(rows_piece.shape[0], 3, head_cols)
    grad_qkv = jnp.transpose(core_return(rows_piece, 2, 0), (1, 0, 2)).astype(f32)

    weight_r = [jnp.concatenate([qkv_full[r][i] for i in range(3)], axis=1) for r in (0, 1)]

    def stream_part(h):
        rows = slice(h * 2 * share, (h + 1) * 2 * share)
        return (nt(grad_proj[0][rows], weight_r[0]) + nt(grad_proj[1][rows], weight_r[1])).astype(bf16)

    grad_proj[1] = after(grad_proj[1], gate_swapped)
    far = after(chip_sum(stream_part(1)), upper_swapped)
    near = after(stream_part(0), qkv_sum[1])
    grad_stream = (deep_alpha * grad_resid_one + team_scatter(near, far)).astype(bf16)
    qkv_bias_part = jnp.zeros((3, width), f32)
    for r in (0, 1):
        part = jnp.sum(grad_proj[r].astype(f32), axis=0).reshape(3, head_cols)
        at = ((zh ^ r) * 2 + zl) * quarter + c * head_cols
        qkv_bias_part = lax.dynamic_update_slice(qkv_bias_part, part, (0, at))
    square_sums = jnp.stack(
        [
            jnp.sum(live * resid_one * resid_one),
            jnp.sum(live * branch * branch),
            jnp.sum(live * ffn * ffn),
            jnp.sum(live) * width,
        ]
    )
    norm_parts = jnp.stack([gain_one_part, bias_one_part, gain_two_part, bias_two_part])
    sums = jnp.concatenate([norm_parts, qkv_bias_part, jnp.pad(square_sums[None], ((0, 0), (0, width - 4)))])
    sums = after(sums, qkv_swapped, grad_stream)
    for axis in TEAM:
        sums = sums + swap(sums, axis)
    if square:
        for axis in plane:
            sums = sums + swap(sums, axis)
    else:
        sums = lax.psum(sums, plane)
    grad_stream = return_rows(after(grad_stream, out_swapped))

    mine = lax.dynamic_slice_in_dim(sums[:7], (zh * 2 + zl) * quarter, quarter, 1)
    stream_stats = jnp.sqrt(sums[7, :3] / sums[7, 3])

    grad_up = jnp.stack([grad_gate_w, grad_upper_w]).astype(bf16)
    grad_up = jnp.transpose(grad_up, (2, 0, 1)).astype(f32)
    return (
        output,
        grad_stream,
        grad_qkv,
        mine[4:7],
        grad_out.astype(f32),
        mine[0],
        mine[1],
        grad_up,
        grad_down.astype(f32),
        mine[2],
        mine[3],
        stream_stats,
    )


def solution(mesh):
    wide, narrow = mesh.shape["wide"], mesh.shape["narrow"]
    square = wide == 8
    if square:
        plane, dims = ("y", "x"), (2, 2)
    else:
        plane, dims = ("plane",), (wide // 2,)
    fine = Mesh(mesh.devices.reshape(dims + (2, 2, narrow // 2)), plane + TEAM)
    w, n = plane + ("core",), ("zh", "zl")
    placed = (
        P(w, n),
        P(w),
        P(w),
        P(None, w, n),
        P(None, n),
        P(n, w),
        P(n),
        P(n),
        P(w, None, n),
        P(n, w),
        P(n),
        P(n),
        P(w, n),
    )
    return jax.shard_map(
        functools.partial(body, square),
        mesh=fine,
        in_specs=placed,
        out_specs=(
            P(w, n),
            P(w, n),
            P(None, w, n),
            P(None, n),
            P(n, w),
            P(n),
            P(n),
            P(w, None, n),
            P(n, w),
            P(n),
            P(n),
            P(),
        ),
        check_vma=False,
    )
```
